32 devices in a mesh: groups: 2 (over x), seq: 16 (over z, y, core).
Axes of the slice: x: 2, y: 2, z: 4, core: 2. Of those that a mesh axis runs over, the one named last changes fastest.
Arguments:
- queries: bfloat16 [96, 8192], P(('groups', 'seq')), parts along dimension 0, may hold values from -48 to 48
- prompt_of: int32 [96, 1], P(('groups', 'seq')), parts along dimension 0, may hold values from 0 to 1; in each aligned block of 3 rows (0 to 2, 3 to 5, ...) at most 2 rows name the same one
- suffix_cache: bfloat16 [96, 512, 2048], P(('groups', 'seq')), parts along dimension 0, may hold values from -6 to 6
- suffix_blocks: int32 [96], P(('groups', 'seq')), parts along dimension 0, may hold values from 1 to 4
- prompt_cache: bfloat16 [4, 2048, 2048], P('groups', 'seq'), parts along dimension 0, may hold values from -16 to 16
- reward_weight: float32 [8192], replicated, may hold values from -0.4375 to 0.4375
Outputs:
- attended: bfloat16 [96, 8192], P(('groups', 'seq')), parts along dimension 0
- scores: float32 [96], P(('groups', 'seq')), parts along dimension 0
The draws below stay inside these ranges and needn't reach their ends.
There are 2 independent parts, one for each index of `groups`. The reference program is written for one: setup_inputs(seed, part) draws one part's arguments, and reference() takes and returns one part's arrays. A program takes and returns all parts, laid end to end along the dimension named above; an argument that names none is the same for every part. Nothing has to cross between parts.
Inputs may be any that keep to these rules, and one draw needn't show every extreme that they name: `prompt_of`: in each device's aligned block of 3 rows at most 2 candidates name the same prompt.
All inputs are finite; a program needn't handle non-finite values.
Results may differ from the reference program's by a relative error of at most 0.015.
Values may be sent and summed in bfloat16 or wider, within the bound.
No kernel may reach another device: no remote copies, remote signals or barrier semaphores. Data moves between devices by JAX's collectives and lax.ppermute only.
A program may use at most 192 MiB of HBM per device.

```python
import math
import jax
import jax.numpy as jnp
import numpy as np
from jax import lax

HQ = 64
KVH = 8
HD = 128
PROMPT_DEV = 128
PROMPTS = 2
CAND_DEV = 3
CAP = 2
BLOCK = 128
SUF_BLOCKS = 4
CANDS = 48
PROMPT_LEN = 2048
SUF_MAX = 512
N_SEQ = 16


def draw_queries(key, part):
    drawn = jax.random.normal(jax.random.fold_in(key, 101), (CANDS, HQ * HD), jnp.float32)
    return jnp.clip(3.0 * drawn, -15.0, 15.0).astype(jnp.bfloat16)


def draw_prompt_cache(key, part):
    drawn = jnp.clip(jax.random.normal(jax.random.fold_in(key, 202), (PROMPTS, PROMPT_LEN, 2 * KVH * HD), jnp.float32), -6.0, 6.0)
    return drawn.astype(jnp.bfloat16)


def draw_suffix_blocks(key, part):
    counts = jax.random.randint(jax.random.fold_in(key, 303), (CANDS,), 1, SUF_BLOCKS + 1, dtype=jnp.int32)
    return counts.at[0].set(SUF_BLOCKS)


def block_levels(own_key, shape, pieces, low, top_value):
    def one(position, parts):
        draws = jax.random.uniform(jax.random.fold_in(jax.random.fold_in(own_key, 6), position), (parts,), jnp.float32, low / len(pieces), top_value / len(pieces))
        return jnp.repeat(jnp.exp(draws), shape[position] // parts).reshape((-1,) + (1,) * (len(shape) - position - 1))

    loudness = one(*pieces[0])
    for cut in pieces[1:]:
        loudness = loudness * one(*cut)
    return loudness


def routed_block(key, own, number, rows, count, top, reach, skew):
    sequence = jax.random.permutation(key, count)
    packed, usual = load_shares(count, rows * top, reach, skew, True), load_shares(count, rows * top, reach, skew, False)
    places = jnp.arange(count)

    def named(sizes, offset_by):
        used = int((sizes > 0).sum())
        fixed = max(1, used // 4)
        shifted = fixed + (places - fixed + offset_by * (used - fixed)) % max(1, count - fixed)
        return jnp.zeros((count,), jnp.int32).at[sequence[jnp.where(places < fixed, places, shifted)]].set(jnp.asarray(sizes, jnp.int32))

    sizes = jnp.where(number % 4 == 0, named(packed, number // 4), named(usual, number - number // 4 - 1))
    mixed = jax.random.permutation(jax.random.fold_in(own, 3), count)
    source_of, taker = mixed[0:count // 2 * 2:2], mixed[1:count // 2 * 2:2]
    room = jnp.minimum(sizes[source_of] - 1, reach - sizes[taker]) // 2
    room = jnp.where((source_of == sequence[0]) | (taker == sequence[0]) | (sizes[taker] == 0), 0, jnp.maximum(room, 0))
    shifted = jax.random.randint(jax.random.fold_in(own, 4), (count // 2,), 0, 1 << 20) % (room + 1)
    sizes = sizes.at[source_of].add(-shifted).at[taker].add(shifted)
    items = jnp.searchsorted(jnp.cumsum(sizes), jnp.arange(rows * top), side="right").astype(jnp.int32)
    grid = items.reshape(top, rows).T
    grid = grid[jax.random.permutation(jax.random.fold_in(own, 1), rows)]
    offset_by = jax.random.randint(jax.random.fold_in(own, 2), (rows, 1), 0, top)
    return jnp.take_along_axis(grid, (jnp.arange(top)[None, :] + offset_by) % top, axis=1)


def load_shares(amount, total, limit, lean, full):
    weights = [(1 << 20) // math.isqrt(standing ** lean) + 1 for standing in range(1, amount + 1)]
    largest = limit if full else min(limit, max(-(-total // amount), total * weights[0] // sum(weights)))
    least = 1 if total - largest >= amount - 1 else 0
    given, rest = [largest] + [least] * (amount - 1), total - largest - least * (amount - 1)
    while rest > 0:
        free = [i for i in range(1, amount) if given[i] < largest] or [i for i in range(1, amount) if given[i] < limit]
        pool, budget = sum([weights[i] for i in free]), rest
        for i in free:
            extra = min(limit - given[i], max(1, budget * weights[i] // pool), rest)
            given[i] = given[i] + extra
            rest = rest - extra
    return np.array(given)


def noise(rng, dims, spread, limit, cuts=(), kind=jnp.bfloat16):
    entries = spread * jax.random.normal(rng, dims, jnp.float32)
    if cuts:
        entries = entries * block_levels(rng, dims, cuts, -0.22, 0.18)
    return jnp.clip(entries, -limit, limit).astype(kind)


def setup_inputs(seed: int = 0, part: int = 0) -> dict:
    streams_of = jax.random.split(jax.random.key(seed), 7)
    part_splits = jax.random.split(jax.random.fold_in(streams_of[6], part), 7)
    queries = draw_queries(jax.random.fold_in(jax.random.fold_in(streams_of[6], part), 71), part)
    prompt_of_keys = jax.random.split(jax.random.fold_in(part_splits[1], 1), CANDS // CAND_DEV)
    prompt_of_turns = jax.random.permutation(jax.random.fold_in(part_splits[1], 3), CANDS // CAND_DEV)
    prompt_of = jax.vmap(lambda own, number: routed_block(jax.random.fold_in(part_splits[1], 2), own, number, CAND_DEV, PROMPTS, 1, CAP, 1))(prompt_of_keys, prompt_of_turns).reshape((CANDS, 1))
    suffix_cache = noise(part_splits[2], (CANDS, SUF_MAX, 2 * KVH * HD), 1.3, 6.0, ((0, 16),))
    suffix_blocks = draw_suffix_blocks(jax.random.fold_in(jax.random.fold_in(streams_of[6], part), 71), part)
    prompt_cache = draw_prompt_cache(jax.random.fold_in(jax.random.fold_in(streams_of[6], part), 71), part)
    reward_weight = noise(streams_of[5], (HQ * HD,), 0.03, 0.4375, (), jnp.float32)
    return {"queries": queries, "prompt_of": prompt_of, "suffix_cache": suffix_cache, "suffix_blocks": suffix_blocks, "prompt_cache": prompt_cache, "reward_weight": reward_weight}


floor_logit = -1.0e30


def merge_parts(first, second):
    joined = jnp.maximum(first[0], second[0])
    keep = jnp.exp(first[0] - joined)
    take = jnp.exp(second[0] - joined)
    sums = first[1] * keep + second[1] * take
    row_count, heads = joined.shape
    mixes = first[2].reshape(row_count, heads, -1) * keep[:, :, None] + second[2].reshape(row_count, heads, -1) * take[:, :, None]
    return (joined, sums, mixes.reshape(row_count, -1))


def prompt_part(grouped, block_cache):
    kv_width = KVH * HD
    keys = block_cache[:, :kv_width].astype(jnp.float32).reshape(-1, KVH, HD)
    values = block_cache[:, kv_width:].astype(jnp.float32).reshape(-1, KVH, HD)
    logits = jnp.einsum("ckgd,tkd->ckgt", grouped, keys) * (HD ** -0.5)
    maxima = jnp.max(logits, axis=-1)
    exponent = jnp.exp(logits - maxima[..., None])
    totals = jnp.sum(exponent, axis=-1)
    rounded = lax.optimization_barrier(exponent.astype(jnp.bfloat16))
    weights = rounded.astype(jnp.float32)
    weighted = jnp.einsum("ckgt,tkd->ckgd", weights, values)
    row_count = grouped.shape[0]
    return (maxima.reshape(row_count, -1), totals.reshape(row_count, -1), weighted.reshape(row_count, -1))


def suffix_part(item_triple):
    query_row, cache_rows, block_count = item_triple
    kv_width = KVH * HD
    grouped = query_row.astype(jnp.float32).reshape(KVH, HQ // KVH, HD)
    keys = cache_rows[:, :kv_width].astype(jnp.float32).reshape(SUF_MAX, KVH, HD)
    values = cache_rows[:, kv_width:].astype(jnp.float32).reshape(SUF_MAX, KVH, HD)
    logits = jnp.einsum("kgd,tkd->kgt", grouped, keys) * (HD ** -0.5)
    live_mask = (jnp.arange(SUF_MAX, dtype=jnp.int32) < BLOCK * block_count)[None, None, :]
    logits = jnp.where(live_mask, logits, floor_logit)
    maxima = jnp.max(logits, axis=-1)
    exponent = jnp.where(live_mask, jnp.exp(logits - maxima[..., None]), 0.0)
    totals = jnp.sum(exponent, axis=-1)
    rounded = lax.optimization_barrier(exponent.astype(jnp.bfloat16))
    weights = rounded.astype(jnp.float32)
    weighted = jnp.einsum("kgt,tkd->kgd", weights, values)
    return (maxima.reshape(-1), totals.reshape(-1), weighted.reshape(-1))


def reference(queries, prompt_of, suffix_cache, suffix_blocks, prompt_cache, reward_weight):
    cand_rows = queries.shape[0]
    start_state = lax.map(suffix_part, (queries, suffix_cache, suffix_blocks))
    grouped = queries.astype(jnp.float32).reshape(cand_rows, KVH, HQ // KVH, HD)
    prompt_ids = prompt_of[:, 0]

    def visit_block(carried, block_index):
        start_row = (block_index * PROMPT_DEV).astype(jnp.int32)
        block_cache = lax.dynamic_slice_in_dim(prompt_cache, start_row, PROMPT_DEV, axis=1)
        chosen = prompt_part(grouped, block_cache[0])
        for prompt in range(1, PROMPTS):
            partial_value = prompt_part(grouped, block_cache[prompt])
            picked = (prompt_ids == prompt)[:, None]
            chosen = tuple(jnp.where(picked, fresh_part, older_part) for fresh_part, older_part in zip(partial_value, chosen))
        return merge_parts(carried, chosen), None

    final_state, unused = lax.scan(visit_block, start_state, jnp.arange(N_SEQ, dtype=jnp.int32))
    attended_full = final_state[2].reshape(cand_rows, HQ, HD) / final_state[1][:, :, None]
    attended = attended_full.reshape(cand_rows, -1).astype(jnp.bfloat16)
    scores = jnp.sum(attended.astype(jnp.float32) * reward_weight, axis=-1)
    return (attended, scores)
```

```python
import math

import jax
import jax.numpy as jnp
from jax import lax
from jax.experimental import pallas as pl
from jax.experimental.pallas import tpu as pltpu
from jax.sharding import PartitionSpec as P

HD = 128
BLOCK = 128
SLAB = 4
F32 = jnp.float32
BF16 = jnp.bfloat16
floor_logit = -1e30


def vmem_spec():
    return pl.BlockSpec(memory_space=pltpu.VMEM)


def split3(x):
    high = x.astype(BF16).astype(F32)
    rest = x - high
    middle = rest.astype(BF16).astype(F32)
    low = (rest - middle).astype(BF16).astype(F32)
    return [high, middle, low]


def pack_stats(pairs):
    rows = []
    for maximum, total in pairs:
        rows += split3(maximum) + split3(total) + [jnp.zeros((2, HD), F32)]
    return jnp.concatenate(rows, axis=0)


def unpack_stats(stats, k):
    at = 8 * k
    maximum = stats[at : at + 1] + stats[at + 1 : at + 2] + stats[at + 2 : at + 3]
    total = stats[at + 3 : at + 4] + stats[at + 4 : at + 5] + stats[at + 5 : at + 6]
    return maximum, total


def to_lanes(column):
    rows = column.shape[0]
    same = lax.broadcasted_iota(jnp.int32, (rows, HD), 0) == lax.broadcasted_iota(
        jnp.int32, (rows, HD), 1
    )
    return jnp.sum(jnp.where(same, jnp.broadcast_to(column, (rows, HD)), 0.0), axis=0, keepdims=True)


def to_rows(lanes, rows, offset):
    same = lax.broadcasted_iota(jnp.int32, (rows, HD), 0) + offset == lax.broadcasted_iota(
        jnp.int32, (rows, HD), 1
    )
    return jnp.sum(jnp.where(same, jnp.broadcast_to(lanes, (rows, HD)), 0.0), axis=1, keepdims=True)


def prepare(me, queries, prompt_of, prompt_cache, kvq, group):
    cands, width = queries.shape
    heads = width // HD
    prompts, span, kv_width2 = prompt_cache.shape
    kv_width = kv_width2 // 2
    hq = kvq * group
    part_rows = kvq * cands * group + 8
    kvw = kvq * HD

    def kernel(me_ref, q_ref, ids_ref, cache_ref, all_ref, *rest):
        q_out = rest[:SLAB]
        kv_out = rest[SLAB : 2 * SLAB]
        scratch, sem = rest[2 * SLAB :]
        mine = me_ref[0]
        copies = []
        for j in range(SLAB):
            column = pl.multiple_of((mine ^ j) * kvw, kvw)
            for side in range(2):
                copy = pltpu.make_async_copy(
                    cache_ref.at[:, :, pl.ds(side * kv_width + column, kvw)],
                    kv_out[j].at[side],
                    sem.at[j, side],
                )
                copy.start()
                copies.append(copy)
        for h in range(heads):
            scratch[pl.ds(h, cands, stride=heads), :] = q_ref[:, h * HD : (h + 1) * HD].astype(F32)
        all_ref[...] = scratch[...].astype(BF16)
        id_rows = [jnp.full((1, HD), ids_ref[r, 0].astype(F32)) for r in range(cands)]
        id_rows = id_rows + [jnp.zeros((8 - cands, HD), F32)]
        for j in range(SLAB):
            first = (mine ^ j) * hq
            pieces = []
            for k in range(kvq):
                for r in range(cands):
                    at = pl.multiple_of(r * heads + first + k * group, 8)
                    pieces.append(scratch[pl.ds(at, group), :])
            q_out[j][...] = jnp.concatenate(pieces + id_rows, axis=0).astype(BF16)
        for copy in copies:
            copy.wait()

    smem = pl.BlockSpec(memory_space=pltpu.SMEM)
    hbm = pl.BlockSpec(memory_space=pl.ANY)
    out = pl.pallas_call(
        kernel,
        out_shape=[jax.ShapeDtypeStruct((cands * heads, HD), BF16)]
        + [jax.ShapeDtypeStruct((part_rows, HD), BF16)] * SLAB
        + [jax.ShapeDtypeStruct((2, prompts, span, kvw), BF16)] * SLAB,
        in_specs=[smem, vmem_spec(), smem, hbm],
        out_specs=[vmem_spec()] * (1 + SLAB) + [hbm] * SLAB,
        scratch_shapes=[
            pltpu.VMEM((cands * heads, HD), F32),
            pltpu.SemaphoreType.DMA((SLAB, 2)),
        ],
        name="prepare",
    )(me, queries, prompt_of, prompt_cache)
    return out[0], out[1 : 1 + SLAB], out[1 + SLAB :]


def suffix_attend(blocks, rows_q, suffix_cache, kv_heads):
    cands, length, kv_width2 = suffix_cache.shape
    kv_width = kv_width2 // 2
    heads = rows_q.shape[0] // cands
    group = heads // kv_heads

    def kernel(blocks_ref, q_ref, key_ref, value_ref, max_ref, sum_ref, mix_ref):
        q = q_ref[...]
        wide = jnp.concatenate([q] * kv_heads, axis=1)
        diagonal = (
            lax.broadcasted_iota(jnp.int32, (heads, kv_width), 0) // group
            == lax.broadcasted_iota(jnp.int32, (heads, kv_width), 1) // HD
        )
        wide = jnp.where(diagonal, wide, jnp.zeros_like(wide))
        logits = lax.dot_general(
            wide, key_ref[0], (((1,), (1,)), ((), ())), preferred_element_type=F32
        ) * HD ** (-0.5)
        live = (
            lax.broadcasted_iota(jnp.int32, (heads, length), 1)
            < BLOCK * blocks_ref[pl.program_id(0)]
        )
        logits = jnp.where(live, logits, floor_logit)
        maxima = jnp.max(logits, axis=1, keepdims=True)
        exponent = jnp.where(live, jnp.exp(logits - maxima), 0.0)
        totals = jnp.sum(exponent, axis=1, keepdims=True)
        mixed = jnp.dot(exponent.astype(BF16), value_ref[0], preferred_element_type=F32)
        max_ref[...] = jnp.broadcast_to(maxima, (heads, HD))
        sum_ref[...] = jnp.broadcast_to(totals, (heads, HD))
        for k in range(kv_heads):
            mix_ref[k * group : (k + 1) * group, :] = mixed[
                k * group : (k + 1) * group, k * HD : (k + 1) * HD
            ]

    shape = jax.ShapeDtypeStruct((cands * heads, HD), F32)
    row_spec = pl.BlockSpec((heads, HD), lambda c, b: (c, 0))
    return pl.pallas_call(
        kernel,
        out_shape=[shape] * 3,
        grid_spec=pltpu.PrefetchScalarGridSpec(
            num_scalar_prefetch=1,
            grid=(cands,),
            in_specs=[
                row_spec,
                pl.BlockSpec((1, length, kv_width), lambda c, b: (c, 0, 0)),
                pl.BlockSpec((1, length, kv_width), lambda c, b: (c, 0, 1)),
            ],
            out_specs=[row_spec] * 3,
        ),
        cost_estimate=pl.CostEstimate(
            flops=4 * cands * heads * length * kv_width,
            transcendentals=cands * heads * length,
            bytes_accessed=2 * suffix_cache.size,
        ),
        name="suffix",
    )(blocks, rows_q, suffix_cache, suffix_cache)


def prompt_attend(query_blocks, caches, cands, kvq, group):
    stacked = not isinstance(query_blocks, list)
    outer = query_blocks.shape[0] if stacked else len(query_blocks)
    chunk = math.gcd(outer, 4)
    part = cands * group
    part_rows = kvq * part + 8
    block_rows = SLAB * part
    out_rows = kvq * block_rows + 8 * kvq
    prompts, span = caches[0].shape[1:3]
    width = SLAB * span

    def kernel(*refs):
        if stacked:
            q_refs = [refs[0].at[i] for i in range(chunk)]
            cache_refs = refs[1 : 1 + SLAB]
            out_refs = [refs[1 + SLAB].at[i] for i in range(chunk)]
        else:
            q_refs = refs[:chunk]
            cache_refs = refs[chunk : chunk + SLAB]
            out_refs = refs[chunk + SLAB :]
        rows = [q_ref[...].astype(F32) for q_ref in q_refs]
        ids = []
        for i in range(chunk):
            for j in range(SLAB):
                for r in range(cands):
                    at = j * part_rows + kvq * part + r
                    ids.append(jnp.broadcast_to(rows[i][at : at + 1], (group, HD)))
        ids = jnp.concatenate(ids, axis=0)
        ids = jnp.concatenate([ids] * (width // HD), axis=1)
        picked = [ids == float(p) for p in range(prompts)]
        stats = [[] for i in range(chunk)]
        for k in range(kvq):
            q = jnp.concatenate(
                [
                    rows[i][j * part_rows + k * part : j * part_rows + (k + 1) * part]
                    for i in range(chunk)
                    for j in range(SLAB)
                ],
                axis=0,
            ).astype(BF16)
            logits = None
            for p in range(prompts):
                keys = jnp.concatenate(
                    [ref[0, p, :, k * HD : (k + 1) * HD] for ref in cache_refs], axis=0
                )
                one = lax.dot_general(
                    q, keys, (((1,), (1,)), ((), ())), preferred_element_type=F32
                )
                logits = one if logits is None else jnp.where(picked[p], one, logits)
            logits = logits * HD ** (-0.5)
            maxima = jnp.max(logits, axis=1, keepdims=True)
            exponent = jnp.exp(logits - maxima)
            totals = jnp.sum(exponent, axis=1, keepdims=True)
            mixed = None
            for p in range(prompts):
                values = jnp.concatenate(
                    [ref[1, p, :, k * HD : (k + 1) * HD] for ref in cache_refs], axis=0
                )
                weights = jnp.where(picked[p], exponent, 0.0).astype(BF16)
                one = jnp.dot(weights, values, preferred_element_type=F32)
                mixed = one if mixed is None else mixed + one
            for i in range(chunk):
                cut = slice(i * block_rows, (i + 1) * block_rows)
                out_refs[i][k * block_rows : (k + 1) * block_rows, :] = mixed[cut].astype(BF16)
                stats[i].append((to_lanes(maxima[cut]), to_lanes(totals[cut])))
        for i in range(chunk):
            out_refs[i][kvq * block_rows :, :] = pack_stats(stats[i]).astype(BF16)

    if stacked:
        whole = [
            pl.BlockSpec(c.shape, lambda s: (0, 0, 0, 0)) for c in caches
        ]
        return pl.pallas_call(
            kernel,
            out_shape=jax.ShapeDtypeStruct((outer, out_rows, HD), BF16),
            grid=(outer // chunk,),
            in_specs=[pl.BlockSpec((chunk, SLAB * part_rows, HD), lambda s: (s, 0, 0))] + whole,
            out_specs=pl.BlockSpec((chunk, out_rows, HD), lambda s: (s, 0, 0)),
            name="prompt",
        )(query_blocks, *caches)
    return pl.pallas_call(
        kernel,
        out_shape=[jax.ShapeDtypeStruct((out_rows, HD), BF16)] * outer,
        in_specs=[vmem_spec()] * (outer + SLAB),
        out_specs=[vmem_spec()] * outer,
        name="prompt",
    )(*query_blocks, *caches)


def merge(blocks, cands, kvq, group):
    stacked = not isinstance(blocks, list)
    outer = blocks.shape[0] if stacked else len(blocks)
    part = cands * group
    block_rows = SLAB * part
    out_rows = kvq * part + 8 * kvq

    def kernel(*refs):
        if stacked:
            in_refs = [refs[0].at[i] for i in range(outer)]
            out_refs = refs[1:]
        else:
            in_refs = refs[:outer]
            out_refs = refs[outer:]
        stats = [ref[kvq * block_rows :, :].astype(F32) for ref in in_refs]
        merged = []
        for k in range(kvq):
            pairs = [unpack_stats(one, k) for one in stats]
            joined = pairs[0][0]
            for maximum, total in pairs[1:]:
                joined = jnp.maximum(joined, maximum)
            total_all = jnp.zeros((1, HD), F32)
            mixed = jnp.zeros((block_rows, HD), F32)
            for (maximum, total), ref in zip(pairs, in_refs):
                factor = jnp.exp(maximum - joined)
                total_all = total_all + factor * total
                mixed = mixed + to_rows(factor, block_rows, 0) * ref[
                    k * block_rows : (k + 1) * block_rows, :
                ].astype(F32)
            merged.append((joined, total_all))
            for j in range(SLAB):
                out_refs[j][k * part : (k + 1) * part, :] = mixed[
                    j * part : (j + 1) * part
                ].astype(BF16)
        packed = pack_stats(merged).astype(BF16)
        for j in range(SLAB):
            out_refs[j][kvq * part :, :] = packed

    args = [blocks] if stacked else blocks
    return pl.pallas_call(
        kernel,
        out_shape=[jax.ShapeDtypeStruct((out_rows, HD), BF16)] * SLAB,
        in_specs=[vmem_spec()] * len(args),
        out_specs=[vmem_spec()] * SLAB,
        name="merge",
    )(*args)


def finish(me, pieces, suffix_state, reward, cands, kvq, group):
    part = cands * group
    hq = kvq * group
    heads = SLAB * hq

    def kernel(me_ref, *refs):
        piece_refs = refs[:SLAB]
        max_ref, sum_ref, mix_ref, reward_ref, out_ref, score_ref, scratch = refs[SLAB:]
        mine = me_ref[0]
        scores = [jnp.zeros((group, HD), F32) for r in range(cands)]
        for j in range(SLAB):
            first = (mine ^ j) * hq
            stats = piece_refs[j][kvq * part :, :].astype(F32)
            mix = piece_refs[j][: kvq * part, :].astype(F32)
            for k in range(kvq):
                maximum, total = unpack_stats(stats, k)
                maximum = to_rows(maximum, part, j * part)
                total = to_rows(total, part, j * part)
                weight = reward_ref[pl.ds(pl.multiple_of(first + k * group, 8), group), :]
                for r in range(cands):
                    at = pl.ds(pl.multiple_of(r * heads + first + k * group, 8), group)
                    cut = slice(r * group, (r + 1) * group)
                    home_max = max_ref[at, :]
                    here_max = jnp.broadcast_to(maximum[cut], (group, HD))
                    joined = jnp.maximum(home_max, here_max)
                    home = jnp.exp(home_max - joined)
                    here = jnp.exp(here_max - joined)
                    total_all = home * sum_ref[at, :] + here * total[cut]
                    mixed = home * mix_ref[at, :] + here * mix[k * part :][cut]
                    attended = (mixed / total_all).astype(BF16).astype(F32)
                    scratch[at, :] = attended
                    scores[r] = scores[r] + attended * weight
        for h in range(heads):
            out_ref[:, h * HD : (h + 1) * HD] = scratch[pl.ds(h, cands, stride=heads), :].astype(
                BF16
            )
        for r in range(cands):
            score_ref[r] = jnp.sum(scores[r])

    smem = pl.BlockSpec(memory_space=pltpu.SMEM)
    return pl.pallas_call(
        kernel,
        out_shape=[
            jax.ShapeDtypeStruct((cands, heads * HD), BF16),
            jax.ShapeDtypeStruct((cands,), F32),
        ],
        in_specs=[smem] + [vmem_spec()] * (SLAB + 4),
        out_specs=[vmem_spec(), smem],
        scratch_shapes=[pltpu.VMEM((cands * heads, HD), F32)],
        name="finish",
    )(me, *pieces, *suffix_state, reward)


def body(queries, prompt_of, suffix_cache, suffix_blocks, prompt_cache, reward_weight):
    cands = queries.shape[0]
    heads = queries.shape[1] // HD
    kv_heads = prompt_cache.shape[2] // (2 * HD)
    group = heads // kv_heads
    kvq = kv_heads // SLAB
    devices = lax.axis_size("seq")
    outer = devices // SLAB
    me = jnp.reshape(lax.axis_index("seq") % SLAB, (1,)).astype(jnp.int32)

    def hop(x, step):
        return lax.ppermute(x, "seq", [(i, i ^ step) for i in range(devices)])

    direct = outer <= 4 and outer & (outer - 1) == 0
    columns = [[SLAB * z + i for z in range(outer)] for i in range(SLAB)]

    rows_q, q_parts, kv_parts = prepare(me, queries, prompt_of, prompt_cache, kvq, group)
    q_parts = [q_parts[0]] + [hop(q_parts[j], j) for j in range(1, SLAB)]
    kv_parts = [kv_parts[0]] + [hop(kv_parts[j], j) for j in range(1, SLAB)]
    q_slab = jnp.concatenate(q_parts, axis=0)
    rows_q, q_slab = lax.optimization_barrier((rows_q, q_slab))
    suffix_state = suffix_attend(suffix_blocks, rows_q, suffix_cache, kv_heads)
    if direct:
        q_all = [q_slab] + [hop(q_slab, SLAB * i) for i in range(1, outer)]
    else:
        q_all = lax.all_gather(q_slab, "seq", axis_index_groups=columns)
    partial = prompt_attend(q_all, kv_parts, cands, kvq, group)
    if direct:
        partial = [partial[0]] + [hop(partial[i], SLAB * i) for i in range(1, outer)]
    else:
        partial = lax.all_to_all(
            partial, "seq", split_axis=0, concat_axis=0, axis_index_groups=columns, tiled=True
        )
    pieces = merge(partial, cands, kvq, group)
    pieces = [pieces[0]] + [hop(pieces[j], j) for j in range(1, SLAB)]
    reward = reward_weight.reshape(heads, HD)
    return tuple(finish(me, pieces, suffix_state, reward, cands, kvq, group))


def solution(mesh):
    placed = (
        P(("groups", "seq"), None),
        P(("groups", "seq"), None),
        P(("groups", "seq"), None, None),
        P(("groups", "seq")),
        P("groups", "seq", None),
        P(),
    )
    return jax.shard_map(
        body,
        mesh=mesh,
        in_specs=placed,
        out_specs=(P(("groups", "seq"), None), P(("groups", "seq"))),
        check_vma=False,
    )
```

```python
import math

import jax
import jax.numpy as jnp
from jax import lax
from jax.experimental import pallas as pl
from jax.experimental.pallas import tpu as pltpu
from jax.sharding import PartitionSpec as P


HD = 128
BLOCK = 128
SLAB = 4
F32 = jnp.float32
BF16 = jnp.bfloat16
floor_logit = -1e30


def vmem_spec():
    return pl.BlockSpec(memory_space=pltpu.VMEM)


def near(arrays):
    return [pltpu.with_memory_space_constraint(x, pltpu.VMEM) for x in arrays]


def split3(x):
    high = x.astype(BF16).astype(F32)
    rest = x - high
    middle = rest.astype(BF16).astype(F32)
    low = (rest - middle).astype(BF16).astype(F32)
    return [high, middle, low]


def pack_stats(pairs):
    rows = []
    for maximum, total in pairs:
        rows += split3(maximum) + split3(total) + [jnp.zeros((2, HD), F32)]
    return jnp.concatenate(rows, axis=0)


def unpack_stats(stats, k):
    at = 8 * k
    maximum = stats[at : at + 1] + stats[at + 1 : at + 2] + stats[at + 2 : at + 3]
    total = stats[at + 3 : at + 4] + stats[at + 4 : at + 5] + stats[at + 5 : at + 6]
    return maximum, total


def to_lanes(column):
    rows = column.shape[0]
    same = lax.broadcasted_iota(jnp.int32, (rows, HD), 0) == lax.broadcasted_iota(
        jnp.int32, (rows, HD), 1
    )
    return jnp.sum(jnp.where(same, jnp.broadcast_to(column, (rows, HD)), 0.0), axis=0, keepdims=True)


def to_rows(lanes, rows, offset):
    same = lax.broadcasted_iota(jnp.int32, (rows, HD), 0) + offset == lax.broadcasted_iota(
        jnp.int32, (rows, HD), 1
    )
    return jnp.sum(jnp.where(same, jnp.broadcast_to(lanes, (rows, HD)), 0.0), axis=1, keepdims=True)


def prepare(me, queries, prompt_of, prompt_cache, kvq, group):
    cands, width = queries.shape
    heads = width // HD
    prompts, span, kv_width2 = prompt_cache.shape
    kv_width = kv_width2 // 2
    hq = kvq * group
    part_rows = kvq * cands * group + 8
    kvw = kvq * HD

    def kernel(me_ref, q_ref, ids_ref, cache_ref, all_ref, *rest):
        q_out = rest[:SLAB]
        kv_out = rest[SLAB : 2 * SLAB]
        (scratch,) = rest[2 * SLAB :]
        mine = me_ref[0]
        for h in range(heads):
            scratch[pl.ds(h, cands, stride=heads), :] = q_ref[:, h * HD : (h + 1) * HD].astype(F32)
        all_ref[...] = scratch[...].astype(BF16)
        id_rows = [jnp.full((1, HD), ids_ref[r].astype(F32)) for r in range(cands)]
        id_rows = id_rows + [jnp.zeros((8 - cands, HD), F32)]
        for j in range(SLAB):
            first = (mine ^ j) * hq
            pieces = []
            for k in range(kvq):
                for r in range(cands):
                    at = pl.multiple_of(r * heads + first + k * group, 8)
                    pieces.append(scratch[pl.ds(at, group), :])
            q_out[j][...] = jnp.concatenate(pieces + id_rows, axis=0).astype(BF16)
        for j in range(SLAB):
            for side in range(2):
                column = pl.multiple_of(side * kv_width + (mine ^ j) * kvw, kvw)
                kv_out[j][side] = cache_ref[:, :, pl.ds(column, kvw)]

    smem = pl.BlockSpec(memory_space=pltpu.SMEM)
    out = pl.pallas_call(
        kernel,
        out_shape=[pltpu.VMEM((cands * heads, HD), BF16)]
        + [pltpu.VMEM((part_rows, HD), BF16)] * SLAB
        + [pltpu.VMEM((2, prompts, span, kvw), BF16)] * SLAB,
        in_specs=[smem, vmem_spec(), smem, vmem_spec()],
        out_specs=[vmem_spec()] * (1 + 2 * SLAB),
        scratch_shapes=[
            pltpu.VMEM((cands * heads, HD), F32),
        ],
        name="prepare",
    )(me, queries, prompt_of, prompt_cache)
    return out[0], out[1 : 1 + SLAB], out[1 + SLAB :]


def suffix_attend(which, blocks, rows_q, suffix_cache, kv_heads):
    cands, length, kv_width2 = suffix_cache.shape
    kv_width = kv_width2 // 2
    heads = rows_q.shape[0] // cands
    group = heads // kv_heads

    def kernel(blocks_ref, q_ref, cache_ref, max_ref, sum_ref, mix_ref, keys, values, sem):
        fetches = [
            pltpu.make_async_copy(
                cache_ref.at[which, :, side * kv_width : (side + 1) * kv_width], target, sem.at[side]
            )
            for side, target in enumerate((keys, values))
        ]
        for fetch in fetches:
            fetch.start()
        q = q_ref[which * heads : (which + 1) * heads, :]
        wide = jnp.concatenate([q] * kv_heads, axis=1)
        diagonal = (
            lax.broadcasted_iota(jnp.int32, (heads, kv_width), 0) // group
            == lax.broadcasted_iota(jnp.int32, (heads, kv_width), 1) // HD
        )
        wide = jnp.where(diagonal, wide, jnp.zeros_like(wide))
        fetches[0].wait()
        logits = lax.dot_general(
            wide,
            keys[...],
            (((1,), (1,)), ((), ())),
            preferred_element_type=F32,
        ) * HD ** (-0.5)
        live = lax.broadcasted_iota(jnp.int32, (heads, length), 1) < BLOCK * blocks_ref[which]
        logits = jnp.where(live, logits, floor_logit)
        maxima = jnp.max(logits, axis=1, keepdims=True)
        exponent = jnp.where(live, jnp.exp(logits - maxima), 0.0)
        totals = jnp.sum(exponent, axis=1, keepdims=True)
        fetches[1].wait()
        mixed = jnp.dot(exponent.astype(BF16), values[...], preferred_element_type=F32)
        max_ref[...] = jnp.broadcast_to(maxima, (heads, HD))
        sum_ref[...] = jnp.broadcast_to(totals, (heads, HD))
        for k in range(kv_heads):
            mix_ref[k * group : (k + 1) * group, :] = mixed[
                k * group : (k + 1) * group, k * HD : (k + 1) * HD
            ]

    return pl.pallas_call(
        kernel,
        out_shape=[pltpu.VMEM((heads, HD), F32)] * 3,
        in_specs=[
            pl.BlockSpec(memory_space=pltpu.SMEM),
            vmem_spec(),
            pl.BlockSpec(memory_space=pl.ANY),
        ],
        out_specs=[vmem_spec()] * 3,
        scratch_shapes=[
            pltpu.VMEM((length, kv_width), BF16),
            pltpu.VMEM((length, kv_width), BF16),
            pltpu.SemaphoreType.DMA((2,)),
        ],
        cost_estimate=pl.CostEstimate(
            flops=4 * heads * length * kv_width,
            transcendentals=heads * length,
            bytes_accessed=2 * suffix_cache.size // cands,
        ),
        name="suffix",
    )(blocks, *near([rows_q]), suffix_cache)


def prompt_attend(query_blocks, caches, cands, kvq, group):
    stacked = not isinstance(query_blocks, list)
    outer = query_blocks.shape[0] if stacked else len(query_blocks)
    chunk = math.gcd(outer, 4)
    part = cands * group
    part_rows = kvq * part + 8
    block_rows = SLAB * part
    out_rows = kvq * block_rows + 8 * kvq
    prompts, span = caches[0].shape[1:3]
    width = SLAB * span

    def kernel(*refs):
        if stacked:
            q_refs = [refs[0].at[i] for i in range(chunk)]
            cache_refs = refs[1 : 1 + SLAB]
            out_refs = [refs[1 + SLAB].at[i] for i in range(chunk)]
        else:
            q_refs = refs[:chunk]
            cache_refs = refs[chunk : chunk + SLAB]
            out_refs = refs[chunk + SLAB :]
        rows = [q_ref[...].astype(F32) for q_ref in q_refs]
        ids = []
        for i in range(chunk):
            for j in range(SLAB):
                for r in range(cands):
                    at = j * part_rows + kvq * part + r
                    ids.append(jnp.broadcast_to(rows[i][at : at + 1], (group, HD)))
        ids = jnp.concatenate(ids, axis=0)
        ids = jnp.concatenate([ids] * (width // HD), axis=1)
        picked = [ids == float(p) for p in range(prompts)]
        stats = [[] for _ in range(chunk)]
        for k in range(kvq):
            q = jnp.concatenate(
                [
                    rows[i][j * part_rows + k * part : j * part_rows + (k + 1) * part]
                    for i in range(chunk)
                    for j in range(SLAB)
                ],
                axis=0,
            ).astype(BF16)
            logits = None
            for p in range(prompts):
                keys = jnp.concatenate(
                    [ref[0, p, :, k * HD : (k + 1) * HD] for ref in cache_refs], axis=0
                )
                one = lax.dot_general(
                    q, keys, (((1,), (1,)), ((), ())), preferred_element_type=F32
                )
                logits = one if logits is None else jnp.where(picked[p], one, logits)
            logits = logits * HD ** (-0.5)
            maxima = jnp.max(logits, axis=1, keepdims=True)
            exponent = jnp.exp(logits - maxima)
            totals = jnp.sum(exponent, axis=1, keepdims=True)
            mixed = None
            for p in range(prompts):
                values = jnp.concatenate(
                    [ref[1, p, :, k * HD : (k + 1) * HD] for ref in cache_refs], axis=0
                )
                weights = jnp.where(picked[p], exponent, 0.0).astype(BF16)
                one = jnp.dot(weights, values, preferred_element_type=F32)
                mixed = one if mixed is None else mixed + one
            for i in range(chunk):
                cut = slice(i * block_rows, (i + 1) * block_rows)
                out_refs[i][k * block_rows : (k + 1) * block_rows, :] = mixed[cut].astype(BF16)
                stats[i].append((to_lanes(maxima[cut]), to_lanes(totals[cut])))
        for i in range(chunk):
            out_refs[i][kvq * block_rows :, :] = pack_stats(stats[i]).astype(BF16)

    if stacked:
        whole = [
            pl.BlockSpec(c.shape, lambda s: (0, 0, 0, 0)) for c in caches
        ]
        return pl.pallas_call(
            kernel,
            out_shape=jax.ShapeDtypeStruct((outer, out_rows, HD), BF16),
            grid=(outer // chunk,),
            in_specs=[pl.BlockSpec((chunk, SLAB * part_rows, HD), lambda s: (s, 0, 0))] + whole,
            out_specs=pl.BlockSpec((chunk, out_rows, HD), lambda s: (s, 0, 0)),
            name="prompt",
        )(query_blocks, *caches)
    return pl.pallas_call(
        kernel,
        out_shape=[pltpu.VMEM((out_rows, HD), BF16)] * outer,
        in_specs=[vmem_spec()] * (outer + SLAB),
        out_specs=[vmem_spec()] * outer,
        name="prompt",
    )(*near(query_blocks), *near(caches))


def merge(blocks, cands, kvq, group):
    stacked = not isinstance(blocks, list)
    outer = blocks.shape[0] if stacked else len(blocks)
    part = cands * group
    block_rows = SLAB * part
    out_rows = kvq * part + 8 * kvq

    def kernel(*refs):
        if stacked:
            in_refs = [refs[0].at[i] for i in range(outer)]
            out_refs = refs[1:]
        else:
            in_refs = refs[:outer]
            out_refs = refs[outer:]
        stats = [ref[kvq * block_rows :, :].astype(F32) for ref in in_refs]
        merged = []
        for k in range(kvq):
            pairs = [unpack_stats(one, k) for one in stats]
            joined = pairs[0][0]
            for maximum, total in pairs[1:]:
                joined = jnp.maximum(joined, maximum)
            total_all = jnp.zeros((1, HD), F32)
            mixed = jnp.zeros((block_rows, HD), F32)
            for (maximum, total), ref in zip(pairs, in_refs):
                factor = jnp.exp(maximum - joined)
                total_all = total_all + factor * total
                mixed = mixed + to_rows(factor, block_rows, 0) * ref[
                    k * block_rows : (k + 1) * block_rows, :
                ].astype(F32)
            merged.append((joined, total_all))
            for j in range(SLAB):
                out_refs[j][k * part : (k + 1) * part, :] = mixed[
                    j * part : (j + 1) * part
                ].astype(BF16)
        packed = pack_stats(merged).astype(BF16)
        for j in range(SLAB):
            out_refs[j][kvq * part :, :] = packed

    args = [blocks] if stacked else blocks
    return pl.pallas_call(
        kernel,
        out_shape=[pltpu.VMEM((out_rows, HD), BF16)] * SLAB,
        in_specs=[vmem_spec()] * len(args),
        out_specs=[vmem_spec()] * SLAB,
        name="merge",
    )(*near(args))


def finish(me, pieces, suffix_state, reward, cands, kvq, group):
    part = cands * group
    hq = kvq * group
    heads = SLAB * hq

    def kernel(me_ref, *refs):
        piece_refs = refs[:SLAB]
        state_refs = refs[SLAB : SLAB + 3 * cands]
        reward_ref, out_ref, score_ref, scratch = refs[SLAB + 3 * cands :]
        mine = me_ref[0]
        scores = [jnp.zeros((group, HD), F32) for _ in range(cands)]
        for j in range(SLAB):
            first = (mine ^ j) * hq
            stats = piece_refs[j][kvq * part :, :].astype(F32)
            mix = piece_refs[j][: kvq * part, :].astype(F32)
            for k in range(kvq):
                maximum, total = unpack_stats(stats, k)
                maximum = to_rows(maximum, part, j * part)
                total = to_rows(total, part, j * part)
                weight = reward_ref[pl.ds(pl.multiple_of(first + k * group, 8), group), :]
                for r in range(cands):
                    max_ref, sum_ref, mix_ref = state_refs[3 * r : 3 * r + 3]
                    at = pl.ds(pl.multiple_of(first + k * group, 8), group)
                    row = pl.ds(pl.multiple_of(r * heads + first + k * group, 8), group)
                    cut = slice(r * group, (r + 1) * group)
                    home_max = max_ref[at, :]
                    here_max = jnp.broadcast_to(maximum[cut], (group, HD))
                    joined = jnp.maximum(home_max, here_max)
                    home = jnp.exp(home_max - joined)
                    here = jnp.exp(here_max - joined)
                    total_all = home * sum_ref[at, :] + here * total[cut]
                    mixed = home * mix_ref[at, :] + here * mix[k * part :][cut]
                    attended = (mixed / total_all).astype(BF16).astype(F32)
                    scratch[row, :] = attended
                    scores[r] = scores[r] + attended * weight
        for h in range(heads):
            out_ref[:, h * HD : (h + 1) * HD] = scratch[pl.ds(h, cands, stride=heads), :].astype(
                BF16
            )
        for r in range(cands):
            score_ref[r] = jnp.sum(scores[r])

    smem = pl.BlockSpec(memory_space=pltpu.SMEM)
    return pl.pallas_call(
        kernel,
        out_shape=[
            jax.ShapeDtypeStruct((cands, heads * HD), BF16),
            jax.ShapeDtypeStruct((cands,), F32),
        ],
        in_specs=[smem] + [vmem_spec()] * (SLAB + 3 * cands + 1),
        out_specs=[vmem_spec(), smem],
        scratch_shapes=[pltpu.VMEM((cands * heads, HD), F32)],
        name="finish",
    )(me, *near(pieces), *near(suffix_state), reward)


def attend(queries, prompt_of, suffix_cache, suffix_blocks, prompt_cache, reward_weight):
    cands = queries.shape[0]
    heads = queries.shape[1] // HD
    kv_heads = prompt_cache.shape[2] // (2 * HD)
    group = heads // kv_heads
    kvq = kv_heads // SLAB
    devices = lax.axis_size("seq")
    outer = devices // SLAB
    me = jnp.reshape(lax.axis_index("seq") % SLAB, (1,)).astype(jnp.int32)

    def hop(x, step):
        return lax.ppermute(x, "seq", [(i, i ^ step) for i in range(devices)])

    def spread(arrays, step):
        return [arrays[0]] + [hop(arrays[i], step * i) for i in range(1, len(arrays))]

    direct = is_direct(devices)
    columns = [[SLAB * z + i for z in range(outer)] for i in range(SLAB)]

    rows_q, q_parts, kv_parts = prepare(me, queries, prompt_of[:, 0], prompt_cache, kvq, group)
    q_parts = spread(q_parts, 1)
    kv_parts = spread(kv_parts, 1)
    q_slab = jnp.concatenate(q_parts, axis=0)
    suffix_state = []
    for c in range(cands):
        suffix_state += suffix_attend(c, suffix_blocks, rows_q, suffix_cache, kv_heads)
    if direct:
        q_all = spread([q_slab] * outer, SLAB)
    else:
        q_all = lax.all_gather(q_slab, "seq", axis_index_groups=columns)
    partial = prompt_attend(q_all, kv_parts, cands, kvq, group)
    if direct:
        partial = spread(partial, SLAB)
    else:
        partial = lax.all_to_all(
            partial, "seq", split_axis=0, concat_axis=0, axis_index_groups=columns, tiled=True
        )
    pieces = spread(merge(partial, cands, kvq, group), 1)
    reward = reward_weight.reshape(heads, HD)
    return tuple(finish(me, pieces, suffix_state, reward, cands, kvq, group))


def is_direct(devices):
    outer = devices // SLAB
    return outer == 4


def solution(mesh):
    placed = (
        P(("groups", "seq"), None),
        P(("groups", "seq"), None),
        P(("groups", "seq"), None, None),
        P(("groups", "seq")),
        P("groups", "seq", None),
        P(),
    )
    return jax.shard_map(
        attend,
        mesh=mesh,
        in_specs=placed,
        out_specs=(P(("groups", "seq"), None), P(("groups", "seq"))),
        check_vma=False,
    )
```

```python
import math

import jax
import jax.numpy as jnp
from jax import lax
from jax.experimental import pallas as pl
from jax.experimental.pallas import tpu as pltpu
from jax.sharding import PartitionSpec as P


HD = 128
BLOCK = 128

SLAB = 4
F32 = jnp.float32
BF16 = jnp.bfloat16
floor_logit = -1e30


def vmem_spec():
    return pl.BlockSpec(memory_space=pltpu.VMEM)


def near(arrays):
    return [pltpu.with_memory_space_constraint(x, pltpu.VMEM) for x in arrays]


def split3(x):
    high = x.astype(BF16).astype(F32)
    rest = x - high
    middle = rest.astype(BF16).astype(F32)
    low = (rest - middle).astype(BF16).astype(F32)
    return [high, middle, low]


def pack_stats(pairs):
    rows = []
    for shift, total in pairs:
        rows += [shift] + split3(total)
    rows += [jnp.zeros((1, HD), F32)] * (stat_rows(len(pairs)) - len(rows))
    return jnp.concatenate(rows, axis=0)


def stat_rows(kvq):
    return -(-4 * kvq // 8) * 8


def unpack_stats(stats, k):
    at = 4 * k
    total = stats[at + 1 : at + 2] + stats[at + 2 : at + 3] + stats[at + 3 : at + 4]
    return stats[at : at + 1], total


def to_lanes(column):
    rows = column.shape[0]
    same = lax.broadcasted_iota(jnp.int32, (rows, HD), 0) == lax.broadcasted_iota(
        jnp.int32, (rows, HD), 1
    )
    return jnp.sum(jnp.where(same, jnp.broadcast_to(column, (rows, HD)), 0.0), axis=0, keepdims=True)


def to_rows(lanes, rows, offset):
    same = lax.broadcasted_iota(jnp.int32, (rows, HD), 0) + offset == lax.broadcasted_iota(
        jnp.int32, (rows, HD), 1
    )
    return jnp.sum(jnp.where(same, jnp.broadcast_to(lanes, (rows, HD)), 0.0), axis=1, keepdims=True)


def prepare(queries, prompt_of, blocks, prompt_cache, kvq, group):
    cands, width = queries.shape
    heads = width // HD
    prompts, span, kv_width2 = prompt_cache.shape
    kv_width = kv_width2 // 2
    hq = kvq * group
    part_rows = kvq * cands * group + 8
    kvw = kvq * HD

    def kernel(q_ref, ids_ref, blocks_ref, cache_ref, all_ref, live_ref, *rest):
        q_out = rest[:SLAB]
        kv_out = rest[SLAB : 2 * SLAB]
        scratch, held, sem = rest[2 * SLAB :]
        mine = lax.axis_index("seq") % SLAB
        fetches = []
        for p in range(prompts):
            fetch = pltpu.make_async_copy(cache_ref.at[p], held.at[p], sem.at[p])
            fetch.start()
            fetches.append(fetch)
        for h in range(heads):
            scratch[pl.ds(h, cands, stride=heads), :] = q_ref[:, h * HD : (h + 1) * HD].astype(F32)
        all_ref[...] = scratch[...].astype(BF16)
        id_rows = [jnp.full((1, HD), ids_ref[r].astype(F32)) for r in range(cands)]
        id_rows = id_rows + [jnp.zeros((8 - cands, HD), F32)]
        for r in range(cands):
            live_ref[r : r + 1, :] = jnp.full((1, HD), BLOCK * blocks_ref[r])
        for j in range(SLAB):
            first = (mine ^ j) * hq
            pieces = []
            for k in range(kvq):
                for r in range(cands):
                    at = pl.multiple_of(r * heads + first + k * group, 8)
                    pieces.append(scratch[pl.ds(at, group), :])
            q_out[j][...] = jnp.concatenate(pieces + id_rows, axis=0).astype(BF16)
        for p in range(prompts):
            fetches[p].wait()
            for j in range(SLAB):
                for side in range(2):
                    column = pl.multiple_of(side * kv_width + (mine ^ j) * kvw, kvw)
                    kv_out[j][side, p] = held[p, :, pl.ds(column, kvw)]

    smem = pl.BlockSpec(memory_space=pltpu.SMEM)
    out = pl.pallas_call(
        kernel,
        out_shape=[pltpu.VMEM((cands * heads, HD), BF16), pltpu.VMEM((8, HD), jnp.int32)]
        + [pltpu.VMEM((part_rows, HD), BF16)] * SLAB
        + [pltpu.VMEM((2, prompts, span, kvw), BF16)] * SLAB,
        in_specs=[vmem_spec(), smem, smem, pl.BlockSpec(memory_space=pl.ANY)],
        out_specs=[vmem_spec()] * (2 + 2 * SLAB),
        scratch_shapes=[
            pltpu.VMEM((cands * heads, HD), F32),
            pltpu.VMEM((prompts, span, kv_width2), BF16),
            pltpu.SemaphoreType.DMA((prompts,)),
        ],
        name="prepare",
    )(queries, prompt_of, blocks, prompt_cache)
    return out[0], out[1], out[2 : 2 + SLAB], out[2 + SLAB :]


def suffix_attend(live, rows_q, suffix_cache, kv_heads):
    cands, length, kv_width2 = suffix_cache.shape
    kv_width = kv_width2 // 2
    heads = rows_q.shape[0] // cands
    group = heads // kv_heads

    def kernel(live_ref, q_ref, cache_ref, max_ref, sum_ref, mix_ref, keys, values, sem):
        fetches = []
        for c in range(cands):
            for side, target in enumerate((keys, values)):
                fetch = pltpu.make_async_copy(
                    cache_ref.at[c, :, side * kv_width : (side + 1) * kv_width],
                    target.at[c],
                    sem.at[c, side],
                )
                fetch.start()
                fetches.append(fetch)
        diagonal = (
            lax.broadcasted_iota(jnp.int32, (heads, kv_width), 0) // group
            == lax.broadcasted_iota(jnp.int32, (heads, kv_width), 1) // HD
        )
        position = lax.broadcasted_iota(jnp.int32, (heads, length), 1)
        for c in range(cands):
            rows = slice(c * heads, (c + 1) * heads)
            wide = jnp.concatenate([q_ref[rows, :]] * kv_heads, axis=1)
            wide = jnp.where(diagonal, wide, jnp.zeros_like(wide))
            fetches[2 * c].wait()
            logits = lax.dot_general(
                wide, keys[c], (((1,), (1,)), ((), ())), preferred_element_type=F32
            ) * HD ** (-0.5)
            live_row = jnp.concatenate([live_ref[c : c + 1, :]] * (length // HD), axis=1)
            live = position < live_row
            logits = jnp.where(live, logits, floor_logit)
            maxima = jnp.max(logits, axis=1, keepdims=True)
            exponent = jnp.where(live, jnp.exp(logits - maxima), 0.0)
            totals = jnp.sum(exponent, axis=1, keepdims=True)
            fetches[2 * c + 1].wait()
            mixed = jnp.dot(exponent.astype(BF16), values[c], preferred_element_type=F32)
            max_ref[rows, :] = jnp.broadcast_to(maxima, (heads, HD))
            sum_ref[rows, :] = jnp.broadcast_to(totals, (heads, HD))
            for k in range(kv_heads):
                at = c * heads + k * group
                mix_ref[at : at + group, :] = mixed[
                    k * group : (k + 1) * group, k * HD : (k + 1) * HD
                ]

    return pl.pallas_call(
        kernel,
        out_shape=[pltpu.VMEM((cands * heads, HD), F32)] * 3,
        in_specs=[vmem_spec(), vmem_spec(), pl.BlockSpec(memory_space=pl.ANY)],
        out_specs=[vmem_spec()] * 3,
        scratch_shapes=[
            pltpu.VMEM((cands, length, kv_width), BF16),
            pltpu.VMEM((cands, length, kv_width), BF16),
            pltpu.SemaphoreType.DMA((cands, 2)),
        ],
        cost_estimate=pl.CostEstimate(
            flops=4 * cands * heads * length * kv_width,
            transcendentals=cands * heads * length,
            bytes_accessed=2 * suffix_cache.size,
        ),
        name="suffix",
    )(*near([live, rows_q]), suffix_cache)


def prompt_attend(query_blocks, caches, cands, kvq, group):
    stacked = not isinstance(query_blocks, list)
    outer = query_blocks.shape[0] if stacked else len(query_blocks)
    chunk = math.gcd(outer, 4)
    part = cands * group
    part_rows = kvq * part + 8
    block_rows = SLAB * part
    out_rows = kvq * block_rows + stat_rows(kvq)
    prompts, _ = caches[0].shape[1:3]

    def kernel(*refs):
        if stacked:
            q_refs = [refs[0].at[i] for i in range(chunk)]
            cache_refs = refs[1 : 1 + SLAB]
            out_refs = [refs[1 + SLAB].at[i] for i in range(chunk)]
        else:
            q_refs = refs[:chunk]
            cache_refs = refs[chunk : chunk + SLAB]
            out_refs = refs[chunk + SLAB :]
        rows = [q_ref[...].astype(F32) for q_ref in q_refs]
        ids = []
        for i in range(chunk):
            for j in range(SLAB):
                for r in range(cands):
                    at = j * part_rows + kvq * part + r
                    ids.append(jnp.broadcast_to(rows[i][at : at + 1], (group, HD)))
        ids = jnp.concatenate(ids, axis=0)
        picked = [ids == float(p) for p in range(prompts)]
        stats = [[] for _ in range(chunk)]
        for k in range(kvq):
            q = jnp.concatenate(
                [
                    rows[i][j * part_rows + k * part : j * part_rows + (k + 1) * part]
                    for i in range(chunk)
                    for j in range(SLAB)
                ],
                axis=0,
            )
            q = jnp.concatenate([jnp.where(one, q, 0.0) for one in picked], axis=1).astype(BF16)

            def both(side):
                return jnp.concatenate(
                    [
                        jnp.concatenate(
                            [ref[side, p, :, k * HD : (k + 1) * HD] for p in range(prompts)], axis=1
                        )
                        for ref in cache_refs
                    ],
                    axis=0,
                )

            logits = lax.dot_general(
                q, both(0), (((1,), (1,)), ((), ())), preferred_element_type=F32
            ) * HD ** (-0.5)
            maxima = jnp.max(logits, axis=1, keepdims=True).astype(BF16).astype(F32)
            exponent = jnp.exp(logits - maxima)
            totals = jnp.sum(exponent, axis=1, keepdims=True)
            wide = jnp.dot(exponent.astype(BF16), both(1), preferred_element_type=F32)
            mixed = wide[:, :HD]
            for p in range(1, prompts):
                mixed = jnp.where(picked[p], wide[:, p * HD : (p + 1) * HD], mixed)
            for i in range(chunk):
                cut = slice(i * block_rows, (i + 1) * block_rows)
                out_refs[i][k * block_rows : (k + 1) * block_rows, :] = mixed[cut].astype(BF16)
                stats[i].append((to_lanes(maxima[cut]), to_lanes(totals[cut])))
        for i in range(chunk):
            out_refs[i][kvq * block_rows :, :] = pack_stats(stats[i]).astype(BF16)

    if stacked:
        whole = [
            pl.BlockSpec(c.shape, lambda s: (0, 0, 0, 0)) for c in caches
        ]
        return pl.pallas_call(
            kernel,
            out_shape=jax.ShapeDtypeStruct((outer, out_rows, HD), BF16),
            grid=(outer // chunk,),
            in_specs=[pl.BlockSpec((chunk, SLAB * part_rows, HD), lambda s: (s, 0, 0))] + whole,
            out_specs=pl.BlockSpec((chunk, out_rows, HD), lambda s: (s, 0, 0)),
            name="prompt",
        )(query_blocks, *caches)
    return pl.pallas_call(
        kernel,
        out_shape=[pltpu.VMEM((out_rows, HD), BF16)] * outer,
        in_specs=[vmem_spec()] * (outer + SLAB),
        out_specs=[vmem_spec()] * outer,
        name="prompt",
    )(*near(query_blocks), *near(caches))


def merge(blocks, cands, kvq, group):
    stacked = not isinstance(blocks, list)
    outer = blocks.shape[0] if stacked else len(blocks)
    part = cands * group
    block_rows = SLAB * part
    out_rows = kvq * part + stat_rows(kvq)

    def kernel(*refs):
        if stacked:
            in_refs = [refs[0].at[i] for i in range(outer)]
            out_refs = refs[1:]
        else:
            in_refs = refs[:outer]
            out_refs = refs[outer:]
        stats = [ref[kvq * block_rows :, :].astype(F32) for ref in in_refs]
        merged = []
        for k in range(kvq):
            pairs = [unpack_stats(one, k) for one in stats]
            joined = pairs[0][0]
            for maximum, total in pairs[1:]:
                joined = jnp.maximum(joined, maximum)
            total_all = jnp.zeros((1, HD), F32)
            mixed = jnp.zeros((block_rows, HD), F32)
            for (maximum, total), ref in zip(pairs, in_refs):
                factor = jnp.exp(maximum - joined)
                total_all = total_all + factor * total
                mixed = mixed + to_rows(factor, block_rows, 0) * ref[
                    k * block_rows : (k + 1) * block_rows, :
                ].astype(F32)
            merged.append((joined, total_all))
            for j in range(SLAB):
                out_refs[j][k * part : (k + 1) * part, :] = mixed[
                    j * part : (j + 1) * part
                ].astype(BF16)
        packed = pack_stats(merged).astype(BF16)
        for j in range(SLAB):
            out_refs[j][kvq * part :, :] = packed

    args = [blocks] if stacked else blocks
    return pl.pallas_call(
        kernel,
        out_shape=[pltpu.VMEM((out_rows, HD), BF16)] * SLAB,
        in_specs=[vmem_spec()] * len(args),
        out_specs=[vmem_spec()] * SLAB,
        name="merge",
    )(*near(args))


def finish(pieces, suffix_state, reward, cands, kvq, group):
    part = cands * group
    hq = kvq * group
    heads = SLAB * hq

    def kernel(*refs):
        piece_refs = refs[:SLAB]
        max_ref, sum_ref, mix_ref, reward_ref, out_ref, score_ref, scratch = refs[SLAB:]
        mine = lax.axis_index("seq") % SLAB
        scores = [jnp.zeros((group, HD), F32) for _ in range(cands)]
        for j in range(SLAB):
            first = (mine ^ j) * hq
            stats = piece_refs[j][kvq * part :, :].astype(F32)
            mix = piece_refs[j][: kvq * part, :].astype(F32)
            for k in range(kvq):
                maximum, total = unpack_stats(stats, k)
                maximum = to_rows(maximum, part, j * part)
                total = to_rows(total, part, j * part)
                weight = reward_ref[pl.ds(pl.multiple_of(first + k * group, 8), group), :]
                for r in range(cands):
                    at = pl.ds(pl.multiple_of(r * heads + first + k * group, 8), group)
                    cut = slice(r * group, (r + 1) * group)
                    home_max = max_ref[at, :]
                    here_max = jnp.broadcast_to(maximum[cut], (group, HD))
                    joined = jnp.maximum(home_max, here_max)
                    home = jnp.exp(home_max - joined)
                    here = jnp.exp(here_max - joined)
                    total_all = home * sum_ref[at, :] + here * total[cut]
                    mixed = home * mix_ref[at, :] + here * mix[k * part :][cut]
                    attended = (mixed / total_all).astype(BF16).astype(F32)
                    scratch[at, :] = attended
                    scores[r] = scores[r] + attended * weight
        for h in range(heads):
            out_ref[:, h * HD : (h + 1) * HD] = scratch[pl.ds(h, cands, stride=heads), :].astype(
                BF16
            )
        for r in range(cands):
            score_ref[r] = jnp.sum(scores[r])

    smem = pl.BlockSpec(memory_space=pltpu.SMEM)
    return pl.pallas_call(
        kernel,
        out_shape=[
            jax.ShapeDtypeStruct((cands, heads * HD), BF16),
            jax.ShapeDtypeStruct((cands,), F32),
        ],
        in_specs=[vmem_spec()] * (SLAB + 4),
        out_specs=[vmem_spec(), smem],
        scratch_shapes=[pltpu.VMEM((cands * heads, HD), F32)],
        name="finish",
    )(*near(pieces), *near(suffix_state), *near([reward]))


def attend(queries, prompt_of, suffix_cache, suffix_blocks, prompt_cache, reward_weight):
    cands = queries.shape[0]
    heads = queries.shape[1] // HD
    kv_heads = prompt_cache.shape[2] // (2 * HD)
    group = heads // kv_heads
    kvq = kv_heads // SLAB
    devices = lax.axis_size("seq")
    outer = devices // SLAB

    def hop(x, step):
        return lax.ppermute(x, "seq", [(i, i ^ step) for i in range(devices)])

    def spread(arrays, step):
        return [arrays[0]] + [hop(arrays[i], step * i) for i in range(1, len(arrays))]

    direct = is_direct(devices)
    columns = [[SLAB * z + i for z in range(outer)] for i in range(SLAB)]

    rows_q, live, q_parts, kv_parts = prepare(
        queries, prompt_of[:, 0], suffix_blocks, prompt_cache, kvq, group
    )
    q_parts = spread(q_parts, 1)
    kv_parts = spread(kv_parts, 1)
    q_slab = jnp.concatenate(q_parts, axis=0)
    suffix_state = suffix_attend(live, rows_q, suffix_cache, kv_heads)
    if direct:
        q_all = spread([q_slab] * outer, SLAB)
    else:
        q_all = lax.all_gather(q_slab, "seq", axis_index_groups=columns)
    partial = prompt_attend(q_all, kv_parts, cands, kvq, group)
    if direct:
        partial = spread(partial, SLAB)
    else:
        partial = lax.all_to_all(
            partial, "seq", split_axis=0, concat_axis=0, axis_index_groups=columns, tiled=True
        )
    pieces = spread(merge(partial, cands, kvq, group), 1)
    reward = reward_weight.reshape(heads, HD)
    return tuple(finish(pieces, suffix_state, reward, cands, kvq, group))


def is_direct(devices):
    outer = devices // SLAB
    return outer == 4


def solution(mesh):
    placed = (
        P(("groups", "seq"), None),
        P(("groups", "seq"), None),
        P(("groups", "seq"), None, None),
        P(("groups", "seq")),
        P("groups", "seq", None),
        P(),
    )
    return jax.shard_map(
        attend,
        mesh=mesh,
        in_specs=placed,
        out_specs=(P(("groups", "seq"), None), P(("groups", "seq"))),
        check_vma=False,
    )
```

```python
import math

import jax
import jax.numpy as jnp
from jax import lax
from jax.experimental import pallas as pl
from jax.experimental.pallas import tpu as pltpu
from jax.sharding import PartitionSpec as P


HD = 128
BLOCK = 128

SLAB = 4
F32 = jnp.float32
BF16 = jnp.bfloat16
floor_logit = -1e30


def vmem_spec():
    return pl.BlockSpec(memory_space=pltpu.VMEM)


def near(arrays):
    return [pltpu.with_memory_space_constraint(x, pltpu.VMEM) for x in arrays]


def split3(x):
    high = x.astype(BF16).astype(F32)
    rest = x - high
    middle = rest.astype(BF16).astype(F32)
    low = (rest - middle).astype(BF16).astype(F32)
    return [high, middle, low]


def pack_stats(pairs):
    rows = []
    for shift, total in pairs:
        rows += [shift] + split3(total)
    rows += [jnp.zeros((1, HD), F32)] * (stat_rows(len(pairs)) - len(rows))
    return jnp.concatenate(rows, axis=0)


def stat_rows(kvq):
    return -(-4 * kvq // 8) * 8


def unpack_stats(stats, k):
    at = 4 * k
    total = stats[at + 1 : at + 2] + stats[at + 2 : at + 3] + stats[at + 3 : at + 4]
    return stats[at : at + 1], total


def to_lanes(column):
    rows = column.shape[0]
    same = lax.broadcasted_iota(jnp.int32, (rows, HD), 0) == lax.broadcasted_iota(
        jnp.int32, (rows, HD), 1
    )
    return jnp.sum(jnp.where(same, jnp.broadcast_to(column, (rows, HD)), 0.0), axis=0, keepdims=True)


def to_rows(lanes, rows, offset):
    same = lax.broadcasted_iota(jnp.int32, (rows, HD), 0) + offset == lax.broadcasted_iota(
        jnp.int32, (rows, HD), 1
    )
    return jnp.sum(jnp.where(same, jnp.broadcast_to(lanes, (rows, HD)), 0.0), axis=1, keepdims=True)


def prepare(queries, prompt_of, blocks, prompt_cache, kvq, group):
    cands, width = queries.shape
    heads = width // HD
    prompts, span, kv_width2 = prompt_cache.shape
    kv_width = kv_width2 // 2
    hq = kvq * group
    part_rows = kvq * cands * group + 8
    kvw = kvq * HD

    def kernel(q_ref, ids_ref, blocks_ref, cache_ref, all_ref, live_ref, *rest):
        own_ref, near_ref, far_ref = rest[:3]
        kv_out = rest[3 : 3 + SLAB]
        (scratch,) = rest[3 + SLAB :]
        mine = lax.axis_index("seq") % SLAB
        for h in range(heads):
            scratch[pl.ds(h, cands, stride=heads), :] = q_ref[:, h * HD : (h + 1) * HD].astype(F32)
        all_ref[...] = scratch[...].astype(BF16)
        id_rows = [jnp.full((1, HD), ids_ref[r].astype(F32)) for r in range(cands)]
        id_rows = id_rows + [jnp.zeros((8 - cands, HD), F32)]
        for r in range(cands):
            live_ref[r : r + 1, :] = jnp.full((1, HD), BLOCK * blocks_ref[r])
        for j in range(SLAB):
            first = (mine ^ j) * hq
            pieces = []
            for k in range(kvq):
                for r in range(cands):
                    at = pl.multiple_of(r * heads + first + k * group, 8)
                    pieces.append(scratch[pl.ds(at, group), :])
            part = jnp.concatenate(pieces + id_rows, axis=0).astype(BF16)
            if j < 2:
                (own_ref, near_ref)[j][...] = part
            else:
                far_ref[(j - 2) * part_rows : (j - 1) * part_rows, :] = part
        for j in range(SLAB):
            for side in range(2):
                column = pl.multiple_of(side * kv_width + (mine ^ j) * kvw, kvw)
                kv_out[j][side] = cache_ref[:, :, pl.ds(column, kvw)]

    smem = pl.BlockSpec(memory_space=pltpu.SMEM)
    out = pl.pallas_call(
        kernel,
        out_shape=[pltpu.VMEM((cands * heads, HD), BF16), pltpu.VMEM((8, HD), jnp.int32)]
        + [pltpu.VMEM((rows, HD), BF16) for rows in (part_rows, part_rows, 2 * part_rows)]
        + [pltpu.VMEM((2, prompts, span, kvw), BF16)] * SLAB,
        in_specs=[vmem_spec(), smem, smem, vmem_spec()],
        out_specs=[vmem_spec()] * (5 + SLAB),
        scratch_shapes=[
            pltpu.VMEM((cands * heads, HD), F32),
        ],
        name="prepare",
    )(queries, prompt_of, blocks, prompt_cache)
    return out[0], out[1], out[2:5], out[5:]


def pack(own, near_part, far, passed):
    rows = own.shape[0]
    half = rows - 8

    def kernel(own_ref, near_ref, far_ref, passed_ref, out_ref):
        segment = lax.broadcasted_iota(jnp.int32, (8, HD), 1) // (HD // SLAB)
        ids = jnp.zeros((8, HD), F32)
        for j, (ref, at) in enumerate(((own_ref, 0), (near_ref, 0), (far_ref, 0), (passed_ref, rows))):
            out_ref[j * half : (j + 1) * half, :] = ref[at : at + half, :]
            ids = jnp.where(segment == j, ref[at + half : at + rows, :].astype(F32), ids)
        out_ref[SLAB * half :, :] = ids.astype(BF16)

    return pl.pallas_call(
        kernel,
        out_shape=pltpu.VMEM((SLAB * half + 8, HD), BF16),
        in_specs=[vmem_spec()] * 4,
        out_specs=vmem_spec(),
        name="pack",
    )(*near([own, near_part, far, passed]))


def suffix_attend(first, count, live, rows_q, suffix_cache, kv_heads):
    cands, length, kv_width2 = suffix_cache.shape
    kv_width = kv_width2 // 2
    heads = rows_q.shape[0] // cands
    group = heads // kv_heads

    def kernel(live_ref, q_ref, cache_ref, max_ref, sum_ref, mix_ref, keys, values, sem):
        fetches = []
        for c in range(count):
            for side, target in enumerate((keys, values)):
                fetch = pltpu.make_async_copy(
                    cache_ref.at[first + c, :, side * kv_width : (side + 1) * kv_width],
                    target.at[c],
                    sem.at[c, side],
                )
                fetch.start()
                fetches.append(fetch)
        diagonal = (
            lax.broadcasted_iota(jnp.int32, (heads, kv_width), 0) // group
            == lax.broadcasted_iota(jnp.int32, (heads, kv_width), 1) // HD
        )
        position = lax.broadcasted_iota(jnp.int32, (heads, length), 1)
        for c in range(count):
            rows = slice(c * heads, (c + 1) * heads)
            held = first * heads
            wide = jnp.concatenate(
                [q_ref[held + c * heads : held + (c + 1) * heads, :]] * kv_heads, axis=1
            )
            wide = jnp.where(diagonal, wide, jnp.zeros_like(wide))
            fetches[2 * c].wait()
            logits = lax.dot_general(
                wide, keys[c], (((1,), (1,)), ((), ())), preferred_element_type=F32
            ) * HD ** (-0.5)
            live_row = jnp.concatenate([live_ref[first + c : first + c + 1, :]] * (length // HD), axis=1)
            live = position < live_row
            logits = jnp.where(live, logits, floor_logit)
            maxima = jnp.max(logits, axis=1, keepdims=True)
            exponent = jnp.where(live, jnp.exp(logits - maxima), 0.0)
            totals = jnp.sum(exponent, axis=1, keepdims=True)
            fetches[2 * c + 1].wait()
            mixed = jnp.dot(exponent.astype(BF16), values[c], preferred_element_type=F32)
            max_ref[rows, :] = jnp.broadcast_to(maxima, (heads, HD))
            sum_ref[rows, :] = jnp.broadcast_to(totals, (heads, HD))
            for k in range(kv_heads):
                at = c * heads + k * group
                mix_ref[at : at + group, :] = mixed[
                    k * group : (k + 1) * group, k * HD : (k + 1) * HD
                ]

    return pl.pallas_call(
        kernel,
        out_shape=[pltpu.VMEM((count * heads, HD), F32)] * 3,
        in_specs=[vmem_spec(), vmem_spec(), pl.BlockSpec(memory_space=pl.ANY)],
        out_specs=[vmem_spec()] * 3,
        scratch_shapes=[
            pltpu.VMEM((count, length, kv_width), BF16),
            pltpu.VMEM((count, length, kv_width), BF16),
            pltpu.SemaphoreType.DMA((count, 2)),
        ],
        cost_estimate=pl.CostEstimate(
            flops=4 * count * heads * length * kv_width,
            transcendentals=count * heads * length,
            bytes_accessed=2 * suffix_cache.size * count // cands,
        ),
        name="suffix",
    )(*near([live, rows_q]), suffix_cache)


def prompt_attend(query_blocks, caches, cands, kvq, group):
    stacked = not isinstance(query_blocks, list)
    outer = query_blocks.shape[0] if stacked else len(query_blocks)
    chunk = math.gcd(outer, 4)
    part = cands * group
    part_rows = kvq * part
    block_rows = SLAB * part
    out_rows = kvq * block_rows + stat_rows(kvq)
    prompts, _ = caches[0].shape[1:3]

    def kernel(*refs):
        if stacked:
            q_refs = [refs[0].at[i] for i in range(chunk)]
            cache_refs = refs[1 : 1 + SLAB]
            out_refs = [refs[1 + SLAB].at[i] for i in range(chunk)]
        else:
            q_refs = refs[:chunk]
            cache_refs = refs[chunk : chunk + SLAB]
            out_refs = refs[chunk + SLAB :]
        rows = [q_ref[...].astype(F32) for q_ref in q_refs]
        ids = []
        segment = lax.broadcasted_iota(jnp.int32, (8, HD), 1) // (HD // SLAB)
        for i in range(chunk):
            for j in range(SLAB):
                mine = jnp.where(segment == j, rows[i][SLAB * part_rows :], 0.0)
                mine = jnp.max(mine, axis=1, keepdims=True)
                for r in range(cands):
                    ids.append(jnp.broadcast_to(mine[r : r + 1], (group, HD)))
        ids = jnp.concatenate(ids, axis=0)
        picked = [ids == float(p) for p in range(prompts)]
        stats = [[] for _ in range(chunk)]
        for k in range(kvq):
            q = jnp.concatenate(
                [
                    rows[i][j * part_rows + k * part : j * part_rows + (k + 1) * part]
                    for i in range(chunk)
                    for j in range(SLAB)
                ],
                axis=0,
            )
            q = jnp.concatenate([jnp.where(one, q, 0.0) for one in picked], axis=1).astype(BF16)

            def both(side):
                return jnp.concatenate(
                    [
                        jnp.concatenate(
                            [ref[side, p, :, k * HD : (k + 1) * HD] for p in range(prompts)], axis=1
                        )
                        for ref in cache_refs
                    ],
                    axis=0,
                )

            logits = lax.dot_general(
                q, both(0), (((1,), (1,)), ((), ())), preferred_element_type=F32
            ) * HD ** (-0.5)
            maxima = jnp.max(logits, axis=1, keepdims=True).astype(BF16).astype(F32)
            exponent = jnp.exp(logits - maxima)
            totals = jnp.sum(exponent, axis=1, keepdims=True)
            wide = jnp.dot(exponent.astype(BF16), both(1), preferred_element_type=F32)
            mixed = wide[:, :HD]
            for p in range(1, prompts):
                mixed = jnp.where(picked[p], wide[:, p * HD : (p + 1) * HD], mixed)
            for i in range(chunk):
                cut = slice(i * block_rows, (i + 1) * block_rows)
                out_refs[i][k * block_rows : (k + 1) * block_rows, :] = mixed[cut].astype(BF16)
                stats[i].append((to_lanes(maxima[cut]), to_lanes(totals[cut])))
        for i in range(chunk):
            out_refs[i][kvq * block_rows :, :] = pack_stats(stats[i]).astype(BF16)

    if stacked:
        whole = [
            pl.BlockSpec(c.shape, lambda s: (0, 0, 0, 0)) for c in caches
        ]
        return pl.pallas_call(
            kernel,
            out_shape=jax.ShapeDtypeStruct((outer, out_rows, HD), BF16),
            grid=(outer // chunk,),
            in_specs=[pl.BlockSpec((chunk, SLAB * part_rows + 8, HD), lambda s: (s, 0, 0))] + whole,
            out_specs=pl.BlockSpec((chunk, out_rows, HD), lambda s: (s, 0, 0)),
            name="prompt",
        )(query_blocks, *caches)
    return pl.pallas_call(
        kernel,
        out_shape=[pltpu.VMEM((out_rows, HD), BF16)] * outer,
        in_specs=[vmem_spec()] * (outer + SLAB),
        out_specs=[vmem_spec()] * outer,
        name="prompt",
    )(*near(query_blocks), *near(caches))


def merge(blocks, cands, kvq, group):
    stacked = not isinstance(blocks, list)
    outer = blocks.shape[0] if stacked else len(blocks)
    part = cands * group
    block_rows = SLAB * part
    out_rows = kvq * part + stat_rows(kvq)

    def kernel(*refs):
        if stacked:
            in_refs = [refs[0].at[i] for i in range(outer)]
            out_refs = refs[1:]
        else:
            in_refs = refs[:outer]
            out_refs = refs[outer:]
        stats = [ref[kvq * block_rows :, :].astype(F32) for ref in in_refs]
        merged = []
        for k in range(kvq):
            pairs = [unpack_stats(one, k) for one in stats]
            joined = pairs[0][0]
            for maximum, total in pairs[1:]:
                joined = jnp.maximum(joined, maximum)
            total_all = jnp.zeros((1, HD), F32)
            mixed = jnp.zeros((block_rows, HD), F32)
            for (maximum, total), ref in zip(pairs, in_refs):
                factor = jnp.exp(maximum - joined)
                total_all = total_all + factor * total
                mixed = mixed + to_rows(factor, block_rows, 0) * ref[
                    k * block_rows : (k + 1) * block_rows, :
                ].astype(F32)
            merged.append((joined, total_all))
            for j in range(SLAB):
                out_refs[j][k * part : (k + 1) * part, :] = mixed[
                    j * part : (j + 1) * part
                ].astype(BF16)
        packed = pack_stats(merged).astype(BF16)
        for j in range(SLAB):
            out_refs[j][kvq * part :, :] = packed

    args = [blocks] if stacked else blocks
    return pl.pallas_call(
        kernel,
        out_shape=[pltpu.VMEM((out_rows, HD), BF16)] * SLAB,
        in_specs=[vmem_spec()] * len(args),
        out_specs=[vmem_spec()] * SLAB,
        name="merge",
    )(*near(args))


def finish(pieces, suffix_state, reward, cands, kvq, group):
    part = cands * group
    hq = kvq * group
    heads = SLAB * hq

    def kernel(*refs):
        piece_refs = refs[:SLAB]
        state_refs = refs[SLAB : SLAB + len(suffix_state)]
        reward_ref, out_ref, score_ref, scratch = refs[SLAB + len(suffix_state) :]
        split = suffix_state[0].shape[0] // heads
        mine = lax.axis_index("seq") % SLAB
        scores = [jnp.zeros((group, HD), F32) for _ in range(cands)]
        for j in range(SLAB):
            first = (mine ^ j) * hq
            piece = piece_refs[j][...].astype(F32)
            mix, stats = piece[: kvq * part], piece[kvq * part :]
            for k in range(kvq):
                maximum, total = unpack_stats(stats, k)
                maximum = to_rows(maximum, part, j * part)
                total = to_rows(total, part, j * part)
                weight = reward_ref[pl.ds(pl.multiple_of(first + k * group, 8), group), :]
                for r in range(cands):
                    base = r * heads if r < split else (r - split) * heads
                    max_ref, sum_ref, mix_ref = state_refs[:3] if r < split else state_refs[3:]
                    row = pl.ds(pl.multiple_of(r * heads + first + k * group, 8), group)
                    at = pl.ds(pl.multiple_of(base + first + k * group, 8), group)
                    cut = slice(r * group, (r + 1) * group)
                    home_max = max_ref[at, :]
                    here_max = jnp.broadcast_to(maximum[cut], (group, HD))
                    joined = jnp.maximum(home_max, here_max)
                    home = jnp.exp(home_max - joined)
                    here = jnp.exp(here_max - joined)
                    total_all = home * sum_ref[at, :] + here * total[cut]
                    mixed = home * mix_ref[at, :] + here * mix[k * part :][cut]
                    attended = (mixed / total_all).astype(BF16).astype(F32)
                    scratch[row, :] = attended
                    scores[r] = scores[r] + attended * weight
        for h in range(heads):
            out_ref[:, h * HD : (h + 1) * HD] = scratch[pl.ds(h, cands, stride=heads), :].astype(
                BF16
            )
        for r in range(cands):
            score_ref[r] = jnp.sum(scores[r])

    smem = pl.BlockSpec(memory_space=pltpu.SMEM)
    return pl.pallas_call(
        kernel,
        out_shape=[
            jax.ShapeDtypeStruct((cands, heads * HD), BF16),
            jax.ShapeDtypeStruct((cands,), F32),
        ],
        in_specs=[vmem_spec()] * (SLAB + len(suffix_state) + 1),
        out_specs=[vmem_spec(), smem],
        scratch_shapes=[pltpu.VMEM((cands * heads, HD), F32)],
        name="finish",
    )(*near(pieces), *near(suffix_state), *near([reward]))


def attend(queries, prompt_of, suffix_cache, suffix_blocks, prompt_cache, reward_weight):
    cands = queries.shape[0]
    heads = queries.shape[1] // HD
    kv_heads = prompt_cache.shape[2] // (2 * HD)
    group = heads // kv_heads
    kvq = kv_heads // SLAB
    devices = lax.axis_size("seq")
    outer = devices // SLAB

    def hop(x, step):
        return lax.ppermute(x, "seq", [(i, i ^ step) for i in range(devices)])

    def spread(arrays, step):
        return [arrays[0]] + [hop(arrays[i], step * i) for i in range(1, len(arrays))]

    def relay(own, near_part, far_part):
        far = hop(far_part, 2)
        return [own, hop(near_part, 1), far, hop(far, 1)]

    direct = is_direct(devices)
    columns = [[SLAB * z + i for z in range(outer)] for i in range(SLAB)]

    rows_q, live, q_parts, kv_parts = prepare(
        queries, prompt_of[:, 0], suffix_blocks, prompt_cache, kvq, group
    )
    kv_parts = spread(kv_parts, 1)
    own, near_q, far_q, passed_q = relay(*q_parts)
    q_slab = pack(own, near_q, far_q, passed_q)
    early = (2 * cands + 2) // 3
    suffix_state = []
    for first, count in ((0, early), (early, cands - early)):
        suffix_state += suffix_attend(first, count, live, rows_q, suffix_cache, kv_heads)
    if direct:
        q_all = spread([q_slab] * outer, SLAB)
    else:
        q_all = lax.all_gather(q_slab, "seq", axis_index_groups=columns)
    partial = prompt_attend(q_all, kv_parts, cands, kvq, group)
    if direct:
        partial = spread(partial, SLAB)
    else:
        partial = lax.all_to_all(
            partial, "seq", split_axis=0, concat_axis=0, axis_index_groups=columns, tiled=True
        )
    pieces = spread(merge(partial, cands, kvq, group), 1)
    reward = reward_weight.reshape(heads, HD)
    return tuple(finish(pieces, suffix_state, reward, cands, kvq, group))


def is_direct(devices):
    outer = devices // SLAB
    return outer == 4


def solution(mesh):
    placed = (
        P(("groups", "seq"), None),
        P(("groups", "seq"), None),
        P(("groups", "seq"), None, None),
        P(("groups", "seq")),
        P("groups", "seq", None),
        P(),
    )
    return jax.shard_map(
        attend,
        mesh=mesh,
        in_specs=placed,
        out_specs=(P(("groups", "seq"), None), P(("groups", "seq"))),
        check_vma=False,
    )
```

```python
import math

import jax
import jax.numpy as jnp
from jax import lax
from jax.experimental import pallas as pl
from jax.experimental.pallas import tpu as pltpu
from jax.sharding import PartitionSpec as P


HD = 128
BLOCK = 128
LOG2E = 1.4426950408889634

SLAB = 4
F32 = jnp.float32
BF16 = jnp.bfloat16
floor_logit = -1e30


def vmem_spec():
    return pl.BlockSpec(memory_space=pltpu.VMEM)


def near(arrays):
    return [pltpu.with_memory_space_constraint(x, pltpu.VMEM) for x in arrays]


def split3(x):
    high = x.astype(BF16).astype(F32)
    rest = x - high
    middle = rest.astype(BF16).astype(F32)
    low = (rest - middle).astype(BF16).astype(F32)
    return [high, middle, low]


def pack_stats(pairs):
    rows = []
    for shift, total in pairs:
        rows += [shift] + split3(total)
    rows += [jnp.zeros((1, HD), F32)] * (stat_rows(len(pairs)) - len(rows))
    return jnp.concatenate(rows, axis=0)


def stat_rows(kvq):
    return -(-4 * kvq // 8) * 8


def unpack_stats(stats, k):
    at = 4 * k
    total = stats[at + 1 : at + 2] + stats[at + 2 : at + 3] + stats[at + 3 : at + 4]
    return stats[at : at + 1], total


def to_lanes(column):
    rows = column.shape[0]
    same = lax.broadcasted_iota(jnp.int32, (rows, HD), 0) == lax.broadcasted_iota(
        jnp.int32, (rows, HD), 1
    )
    return jnp.sum(jnp.where(same, jnp.broadcast_to(column, (rows, HD)), 0.0), axis=0, keepdims=True)


def to_rows(lanes, rows, offset):
    same = lax.broadcasted_iota(jnp.int32, (rows, HD), 0) + offset == lax.broadcasted_iota(
        jnp.int32, (rows, HD), 1
    )
    return jnp.sum(jnp.where(same, jnp.broadcast_to(lanes, (rows, HD)), 0.0), axis=1, keepdims=True)


def prepare(queries, prompt_of, blocks, prompt_cache, kvq, group):
    cands, width = queries.shape
    heads = width // HD
    prompts, span, kv_width2 = prompt_cache.shape
    kv_width = kv_width2 // 2
    hq = kvq * group
    part_rows = kvq * cands * group + 8
    kvw = kvq * HD

    def kernel(q_hbm, ids_hbm, blocks_hbm, cache_ref, *rest):
        all_ref, live_ref, own_ref, near_ref, far_ref = rest[:5]
        kv_out = rest[5:7]
        q_ref, ids_ref, blocks_ref, scratch, sem, kv_sem = rest[7:]
        mine = lax.axis_index("seq") % SLAB
        copies = []
        for j in range(2):
            for side in range(2):
                column = pl.multiple_of(side * kv_width + (mine ^ (2 + j)) * kvw, kvw)
                copy = pltpu.make_async_copy(
                    cache_ref.at[:, :, pl.ds(column, kvw)], kv_out[j].at[side], kv_sem.at[j, side]
                )
                copy.start()
                copies.append(copy)
        q_copy = pltpu.make_async_copy(q_hbm, q_ref, sem.at[0])
        q_copy.start()
        ids_copy = pltpu.make_async_copy(ids_hbm, ids_ref, sem.at[1])
        ids_copy.start()
        blocks_copy = pltpu.make_async_copy(blocks_hbm, blocks_ref, sem.at[2])
        blocks_copy.start()
        q_copy.wait()
        for h in range(heads):
            scratch[pl.ds(h, cands, stride=heads), :] = q_ref[:, h * HD : (h + 1) * HD].astype(F32)
        all_ref[...] = scratch[...].astype(BF16)
        ids_copy.wait()
        blocks_copy.wait()
        for r in range(cands):
            live_ref[r : r + 1, :] = jnp.full((1, HD), BLOCK * blocks_ref[r])
        id_rows = [jnp.full((1, HD), ids_ref[r].astype(F32)) for r in range(cands)]
        id_rows = id_rows + [jnp.zeros((8 - cands, HD), F32)]
        for j in range(SLAB):
            first = (mine ^ j) * hq
            pieces = []
            for k in range(kvq):
                for r in range(cands):
                    at = pl.multiple_of(r * heads + first + k * group, 8)
                    pieces.append(scratch[pl.ds(at, group), :])
            part = jnp.concatenate(pieces + id_rows, axis=0).astype(BF16)
            if j < 2:
                (own_ref, near_ref)[j][...] = part
            else:
                far_ref[(j - 2) * part_rows : (j - 1) * part_rows, :] = part
        for copy in copies:
            copy.wait()

    hbm = pl.BlockSpec(memory_space=pl.ANY)
    out = pl.pallas_call(
        kernel,
        out_shape=[pltpu.VMEM((cands * heads, HD), BF16), pltpu.VMEM((8, HD), jnp.int32)]
        + [pltpu.VMEM((rows, HD), BF16) for rows in (part_rows, part_rows, 2 * part_rows)]
        + [pltpu.VMEM((2, prompts, span, kvw), BF16)] * 2,
        in_specs=[hbm] * 4,
        out_specs=[vmem_spec()] * 7,
        scratch_shapes=[
            pltpu.VMEM((cands, width), BF16),
            pltpu.SMEM((cands,), jnp.int32),
            pltpu.SMEM((cands,), jnp.int32),
            pltpu.VMEM((cands * heads, HD), F32),
            pltpu.SemaphoreType.DMA((3,)),
            pltpu.SemaphoreType.DMA((2, 2)),
        ],
        name="prepare",
    )(queries, prompt_of, blocks, prompt_cache)
    return out[0], out[1], out[2:5], out[5:]


def pack(own, near_part, far, passed):
    rows = own.shape[0]
    half = rows - 8

    def kernel(own_ref, near_ref, far_ref, passed_ref, out_ref):
        segment = lax.broadcasted_iota(jnp.int32, (8, HD), 1) // (HD // SLAB)
        ids = jnp.zeros((8, HD), F32)
        for j, (ref, at) in enumerate(((own_ref, 0), (near_ref, 0), (far_ref, 0), (passed_ref, rows))):
            out_ref[j * half : (j + 1) * half, :] = ref[at : at + half, :]
            ids = jnp.where(segment == j, ref[at + half : at + rows, :].astype(F32), ids)
        out_ref[SLAB * half :, :] = ids.astype(BF16)

    return pl.pallas_call(
        kernel,
        out_shape=pltpu.VMEM((SLAB * half + 8, HD), BF16),
        in_specs=[vmem_spec()] * 4,
        out_specs=vmem_spec(),
        name="pack",
    )(*near([own, near_part, far, passed]))


def suffix_attend(first, count, live, rows_q, suffix_cache, kv_heads, prompt_cache=None):
    cands, length, kv_width2 = suffix_cache.shape
    kv_width = kv_width2 // 2
    heads = rows_q.shape[0] // cands
    group = heads // kv_heads

    keeps = prompt_cache is not None
    if keeps:
        prompts, span, prompt_width2 = prompt_cache.shape
        prompt_width = prompt_width2 // 2
        kvw = prompt_width // SLAB

    def kernel(live_ref, q_ref, cache_ref, *rest):
        if keeps:
            prompt_ref, max_ref, sum_ref, mix_ref, *kv_refs, keys, values, sem, own_sem = rest
        else:
            max_ref, sum_ref, mix_ref, keys, values, sem = rest
        fetches = []
        for c in range(count):
            for side, target in enumerate((keys, values)):
                fetch = pltpu.make_async_copy(
                    cache_ref.at[first + c, :, side * kv_width : (side + 1) * kv_width],
                    target.at[c],
                    sem.at[c, side],
                )
                fetch.start()
                fetches.append(fetch)
        owns = []
        if keeps:
            mine = lax.axis_index("seq") % SLAB
            for j, ref in enumerate(kv_refs):
                for side in range(2):
                    column = pl.multiple_of(side * prompt_width + (mine ^ j) * kvw, kvw)
                    own = pltpu.make_async_copy(
                        prompt_ref.at[:, :, pl.ds(column, kvw)], ref.at[side], own_sem.at[j, side]
                    )
                    own.start()
                    owns.append(own)
        diagonal = (
            lax.broadcasted_iota(jnp.int32, (heads, kv_width), 0) // group
            == lax.broadcasted_iota(jnp.int32, (heads, kv_width), 1) // HD
        )
        position = lax.broadcasted_iota(jnp.int32, (heads, length), 1)
        for c in range(count):
            rows = slice(c * heads, (c + 1) * heads)
            held = first * heads
            wide = jnp.concatenate(
                [q_ref[held + c * heads : held + (c + 1) * heads, :]] * kv_heads, axis=1
            )
            wide = jnp.where(diagonal, wide, jnp.zeros_like(wide))
            fetches[2 * c].wait()
            logits = lax.dot_general(
                wide, keys[c], (((1,), (1,)), ((), ())), preferred_element_type=F32
            ) * (LOG2E * HD ** (-0.5))
            live_row = jnp.concatenate([live_ref[first + c : first + c + 1, :]] * (length // HD), axis=1)
            live = position < live_row
            logits = jnp.where(live, logits, floor_logit)
            maxima = jnp.max(logits, axis=1, keepdims=True)
            exponent = jnp.where(live, jnp.exp2(logits - maxima), 0.0)
            totals = jnp.sum(exponent, axis=1, keepdims=True)
            fetches[2 * c + 1].wait()
            mixed = jnp.dot(exponent.astype(BF16), values[c], preferred_element_type=F32)
            max_ref[rows, :] = jnp.broadcast_to(maxima, (heads, HD))
            sum_ref[rows, :] = jnp.broadcast_to(totals, (heads, HD))
            for k in range(kv_heads):
                at = c * heads + k * group
                mix_ref[at : at + group, :] = mixed[
                    k * group : (k + 1) * group, k * HD : (k + 1) * HD
                ]
        for own in owns:
            own.wait()

    hbm = pl.BlockSpec(memory_space=pl.ANY)
    extra = [pltpu.VMEM((2, prompts, span, kvw), BF16)] * 2 if keeps else []
    return pl.pallas_call(
        kernel,
        out_shape=[pltpu.VMEM((count * heads, HD), F32)] * 3 + extra,
        in_specs=[vmem_spec(), vmem_spec(), hbm] + [hbm] * keeps,
        out_specs=[vmem_spec()] * (3 + len(extra)),
        scratch_shapes=[
            pltpu.VMEM((count, length, kv_width), BF16),
            pltpu.VMEM((count, length, kv_width), BF16),
            pltpu.SemaphoreType.DMA((count, 2)),
        ]
        + [pltpu.SemaphoreType.DMA((2, 2))] * keeps,
        cost_estimate=pl.CostEstimate(
            flops=4 * count * heads * length * kv_width,
            transcendentals=count * heads * length,
            bytes_accessed=2 * suffix_cache.size * count // cands,
        ),
        name="suffix",
    )(*near([live, rows_q]), suffix_cache, *([prompt_cache] if keeps else []))


def prompt_attend(query_blocks, caches, cands, kvq, group):
    stacked = not isinstance(query_blocks, list)
    outer = query_blocks.shape[0] if stacked else len(query_blocks)
    chunk = math.gcd(outer, 4)
    part = cands * group
    part_rows = kvq * part
    block_rows = SLAB * part
    out_rows = kvq * block_rows + stat_rows(kvq)
    prompts, _ = caches[0].shape[1:3]

    def kernel(*refs):
        if stacked:
            q_refs = [refs[0].at[i] for i in range(chunk)]
            cache_refs = refs[1 : 1 + SLAB]
            out_refs = [refs[1 + SLAB].at[i] for i in range(chunk)]
        else:
            q_refs = refs[:chunk]
            cache_refs = refs[chunk : chunk + SLAB]
            out_refs = refs[chunk + SLAB :]
        rows = [q_ref[...].astype(F32) for q_ref in q_refs]
        ids = []
        segment = lax.broadcasted_iota(jnp.int32, (8, HD), 1) // (HD // SLAB)
        for i in range(chunk):
            for j in range(SLAB):
                mine = jnp.where(segment == j, rows[i][SLAB * part_rows :], 0.0)
                mine = jnp.max(mine, axis=1, keepdims=True)
                for r in range(cands):
                    ids.append(jnp.broadcast_to(mine[r : r + 1], (group, HD)))
        ids = jnp.concatenate(ids, axis=0)
        picked = [ids == float(p) for p in range(prompts)]
        stats = [[] for _ in range(chunk)]
        for k in range(kvq):
            q = jnp.concatenate(
                [
                    rows[i][j * part_rows + k * part : j * part_rows + (k + 1) * part]
                    for i in range(chunk)
                    for j in range(SLAB)
                ],
                axis=0,
            )
            q = jnp.concatenate([jnp.where(one, q, 0.0) for one in picked], axis=1).astype(BF16)

            def both(side):
                return jnp.concatenate(
                    [
                        jnp.concatenate(
                            [ref[side, p, :, k * HD : (k + 1) * HD] for p in range(prompts)], axis=1
                        )
                        for ref in cache_refs
                    ],
                    axis=0,
                )

            logits = lax.dot_general(
                q, both(0), (((1,), (1,)), ((), ())), preferred_element_type=F32
            ) * (LOG2E * HD ** (-0.5))
            maxima = jnp.max(logits, axis=1, keepdims=True).astype(BF16).astype(F32)
            exponent = jnp.exp2(logits - maxima)
            totals = jnp.sum(exponent, axis=1, keepdims=True)
            wide = jnp.dot(exponent.astype(BF16), both(1), preferred_element_type=F32)
            mixed = wide[:, :HD]
            for p in range(1, prompts):
                mixed = jnp.where(picked[p], wide[:, p * HD : (p + 1) * HD], mixed)
            for i in range(chunk):
                cut = slice(i * block_rows, (i + 1) * block_rows)
                out_refs[i][k * block_rows : (k + 1) * block_rows, :] = mixed[cut].astype(BF16)
                stats[i].append((to_lanes(maxima[cut]), to_lanes(totals[cut])))
        for i in range(chunk):
            out_refs[i][kvq * block_rows :, :] = pack_stats(stats[i]).astype(BF16)

    if stacked:
        whole = [
            pl.BlockSpec(c.shape, lambda s: (0, 0, 0, 0)) for c in caches
        ]
        return pl.pallas_call(
            kernel,
            out_shape=jax.ShapeDtypeStruct((outer, out_rows, HD), BF16),
            grid=(outer // chunk,),
            in_specs=[pl.BlockSpec((chunk, SLAB * part_rows + 8, HD), lambda s: (s, 0, 0))] + whole,
            out_specs=pl.BlockSpec((chunk, out_rows, HD), lambda s: (s, 0, 0)),
            name="prompt",
        )(query_blocks, *caches)
    return pl.pallas_call(
        kernel,
        out_shape=[pltpu.VMEM((out_rows, HD), BF16)] * outer,
        in_specs=[vmem_spec()] * (outer + SLAB),
        out_specs=[vmem_spec()] * outer,
        name="prompt",
    )(*near(query_blocks), *near(caches))


def merge(blocks, cands, kvq, group):
    stacked = not isinstance(blocks, list)
    outer = blocks.shape[0] if stacked else len(blocks)
    part = cands * group
    block_rows = SLAB * part
    out_rows = kvq * part + stat_rows(kvq)

    def kernel(*refs):
        if stacked:
            in_refs = [refs[0].at[i] for i in range(outer)]
            out_refs = refs[1:]
        else:
            in_refs = refs[:outer]
            out_refs = refs[outer:]
        stats = [ref[kvq * block_rows :, :].astype(F32) for ref in in_refs]
        merged = []
        for k in range(kvq):
            pairs = [unpack_stats(one, k) for one in stats]
            joined = pairs[0][0]
            for maximum, total in pairs[1:]:
                joined = jnp.maximum(joined, maximum)
            total_all = jnp.zeros((1, HD), F32)
            mixed = jnp.zeros((block_rows, HD), F32)
            for (maximum, total), ref in zip(pairs, in_refs):
                factor = jnp.exp2(maximum - joined)
                total_all = total_all + factor * total
                mixed = mixed + to_rows(factor, block_rows, 0) * ref[
                    k * block_rows : (k + 1) * block_rows, :
                ].astype(F32)
            merged.append((joined, total_all))
            for j in range(SLAB):
                out_refs[j][k * part : (k + 1) * part, :] = mixed[
                    j * part : (j + 1) * part
                ].astype(BF16)
        packed = pack_stats(merged).astype(BF16)
        for j in range(SLAB):
            out_refs[j][kvq * part :, :] = packed

    args = [blocks] if stacked else blocks
    return pl.pallas_call(
        kernel,
        out_shape=[pltpu.VMEM((out_rows, HD), BF16)] * SLAB,
        in_specs=[vmem_spec()] * len(args),
        out_specs=[vmem_spec()] * SLAB,
        name="merge",
    )(*near(args))


def finish(pieces, suffix_state, reward, cands, kvq, group):
    part = cands * group
    hq = kvq * group
    heads = SLAB * hq

    def kernel(*refs):
        piece_refs = refs[:SLAB]
        state_refs = refs[SLAB : SLAB + len(suffix_state)]
        reward_ref, out_ref, score_ref, scratch = refs[SLAB + len(suffix_state) :]
        split = suffix_state[0].shape[0] // heads
        mine = lax.axis_index("seq") % SLAB
        scores = [jnp.zeros((group, HD), F32) for _ in range(cands)]
        for j in range(SLAB):
            first = (mine ^ j) * hq
            piece = piece_refs[j][...].astype(F32)
            mix, stats = piece[: kvq * part], piece[kvq * part :]
            for k in range(kvq):
                maximum, total = unpack_stats(stats, k)
                maximum = to_rows(maximum, part, j * part)
                total = to_rows(total, part, j * part)
                weight = reward_ref[pl.ds(pl.multiple_of(first + k * group, 8), group), :]
                for r in range(cands):
                    base = r * heads if r < split else (r - split) * heads
                    max_ref, sum_ref, mix_ref = state_refs[:3] if r < split else state_refs[3:]
                    row = pl.ds(pl.multiple_of(r * heads + first + k * group, 8), group)
                    at = pl.ds(pl.multiple_of(base + first + k * group, 8), group)
                    cut = slice(r * group, (r + 1) * group)
                    home_max = max_ref[at, :]
                    here_max = jnp.broadcast_to(maximum[cut], (group, HD))
                    joined = jnp.maximum(home_max, here_max)
                    home = jnp.exp2(home_max - joined)
                    here = jnp.exp2(here_max - joined)
                    total_all = home * sum_ref[at, :] + here * total[cut]
                    mixed = home * mix_ref[at, :] + here * mix[k * part :][cut]
                    attended = (mixed / total_all).astype(BF16).astype(F32)
                    scratch[row, :] = attended
                    scores[r] = scores[r] + attended * weight
        for h in range(heads):
            out_ref[:, h * HD : (h + 1) * HD] = scratch[pl.ds(h, cands, stride=heads), :].astype(
                BF16
            )
        for r in range(cands):
            score_ref[r] = jnp.sum(scores[r])

    smem = pl.BlockSpec(memory_space=pltpu.SMEM)
    return pl.pallas_call(
        kernel,
        out_shape=[
            jax.ShapeDtypeStruct((cands, heads * HD), BF16),
            jax.ShapeDtypeStruct((cands,), F32),
        ],
        in_specs=[vmem_spec()] * (SLAB + len(suffix_state) + 1),
        out_specs=[vmem_spec(), smem],
        scratch_shapes=[pltpu.VMEM((cands * heads, HD), F32)],
        name="finish",
    )(*near(pieces), *near(suffix_state), *near([reward]))


def attend(queries, prompt_of, suffix_cache, suffix_blocks, prompt_cache, reward_weight):
    cands = queries.shape[0]
    heads = queries.shape[1] // HD
    kv_heads = prompt_cache.shape[2] // (2 * HD)
    group = heads // kv_heads
    kvq = kv_heads // SLAB
    devices = lax.axis_size("seq")
    outer = devices // SLAB

    def hop(x, step):
        return lax.ppermute(x, "seq", [(i, i ^ step) for i in range(devices)])

    def spread(arrays, step):
        return [arrays[0]] + [hop(arrays[i], step * i) for i in range(1, len(arrays))]

    def relay(own, near_part, far_part):
        far = hop(far_part, 2)
        return [own, hop(near_part, 1), far, hop(far, 1)]

    direct = is_direct(devices)
    columns = [[SLAB * z + i for z in range(outer)] for i in range(SLAB)]

    rows_q, live, q_parts, kv_parts = prepare(
        queries, prompt_of[:, 0], suffix_blocks, prompt_cache, kvq, group
    )
    far_kv = [hop(kv_parts[j], 2 + j) for j in range(2)]
    own, near_q, far_q, passed_q = relay(*q_parts)
    q_slab = pack(own, near_q, far_q, passed_q)
    early = (cands + 2) // 3
    *state, own_kv, near_kv = suffix_attend(
        0, early, live, rows_q, suffix_cache, kv_heads, prompt_cache
    )
    state += suffix_attend(early, cands - early, live, rows_q, suffix_cache, kv_heads)
    kv_parts = [own_kv, hop(near_kv, 1)] + far_kv
    if direct:
        q_all = spread([q_slab] * outer, SLAB)
    else:
        q_all = lax.all_gather(q_slab, "seq", axis_index_groups=columns)
    partial = prompt_attend(q_all, kv_parts, cands, kvq, group)
    if direct:
        partial = spread(partial, SLAB)
    else:
        partial = lax.all_to_all(
            partial, "seq", split_axis=0, concat_axis=0, axis_index_groups=columns, tiled=True
        )
    pieces = spread(merge(partial, cands, kvq, group), 1)
    reward = reward_weight.reshape(heads, HD)
    return tuple(finish(pieces, state, reward, cands, kvq, group))


def is_direct(devices):
    outer = devices // SLAB
    return outer == 4


def solution(mesh):
    placed = (
        P(("groups", "seq"), None),
        P(("groups", "seq"), None),
        P(("groups", "seq"), None, None),
        P(("groups", "seq")),
        P("groups", "seq", None),
        P(),
    )
    return jax.shard_map(
        attend,
        mesh=mesh,
        in_specs=placed,
        out_specs=(P(("groups", "seq"), None), P(("groups", "seq"))),
        check_vma=False,
    )
```

```python
import math

import jax
import jax.numpy as jnp
from jax import lax
from jax.experimental import pallas as pl
from jax.experimental.pallas import tpu as pltpu
from jax.sharding import PartitionSpec as P


HD = 128
BLOCK = 128

SLAB = 4
F32 = jnp.float32
BF16 = jnp.bfloat16
floor_logit = -1e30


def vmem_spec():
    return pl.BlockSpec(memory_space=pltpu.VMEM)


def near(arrays):
    return [pltpu.with_memory_space_constraint(x, pltpu.VMEM) for x in arrays]


def split3(x):
    high = x.astype(BF16).astype(F32)
    rest = x - high
    middle = rest.astype(BF16).astype(F32)
    low = (rest - middle).astype(BF16).astype(F32)
    return [high, middle, low]


def pack_stats(pairs):
    rows = []
    for shift, total in pairs:
        rows += [shift] + split3(total)
    rows += [jnp.zeros((1, HD), F32)] * (stat_rows(len(pairs)) - len(rows))
    return jnp.concatenate(rows, axis=0)


def stat_rows(kvq):
    return -(-4 * kvq // 8) * 8


def unpack_stats(stats, k):
    at = 4 * k
    total = stats[at + 1 : at + 2] + stats[at + 2 : at + 3] + stats[at + 3 : at + 4]
    return stats[at : at + 1], total


def to_lanes(column):
    rows = column.shape[0]
    same = lax.broadcasted_iota(jnp.int32, (rows, HD), 0) == lax.broadcasted_iota(
        jnp.int32, (rows, HD), 1
    )
    return jnp.sum(jnp.where(same, jnp.broadcast_to(column, (rows, HD)), 0.0), axis=0, keepdims=True)


def to_rows(lanes, rows, offset):
    same = lax.broadcasted_iota(jnp.int32, (rows, HD), 0) + offset == lax.broadcasted_iota(
        jnp.int32, (rows, HD), 1
    )
    return jnp.sum(jnp.where(same, jnp.broadcast_to(lanes, (rows, HD)), 0.0), axis=1, keepdims=True)


def prepare(queries, prompt_of, blocks, prompt_cache, kvq, group):
    cands, width = queries.shape
    heads = width // HD
    prompts, span, kv_width2 = prompt_cache.shape
    kv_width = kv_width2 // 2
    hq = kvq * group
    part_rows = kvq * cands * group + 8
    kvw = kvq * HD

    def kernel(q_hbm, ids_hbm, blocks_hbm, cache_ref, *rest):
        all_ref, live_ref, own_ref, near_ref, far_ref = rest[:5]
        kv_out = rest[5:7]
        q_ref, ids_ref, blocks_ref, scratch, sem, kv_sem = rest[7:]
        mine = lax.axis_index("seq") % SLAB
        q_copy = pltpu.make_async_copy(q_hbm, q_ref, sem.at[0])
        q_copy.start()
        ids_copy = pltpu.make_async_copy(ids_hbm, ids_ref, sem.at[1])
        ids_copy.start()
        blocks_copy = pltpu.make_async_copy(blocks_hbm, blocks_ref, sem.at[2])
        blocks_copy.start()
        copies = []
        for j in range(2):
            for side in range(2):
                column = pl.multiple_of(side * kv_width + (mine ^ (2 + j)) * kvw, kvw)
                copy = pltpu.make_async_copy(
                    cache_ref.at[:, :, pl.ds(column, kvw)], kv_out[j].at[side], kv_sem.at[j, side]
                )
                copy.start()
                copies.append(copy)
        q_copy.wait()
        for h in range(heads):
            scratch[pl.ds(h, cands, stride=heads), :] = q_ref[:, h * HD : (h + 1) * HD].astype(F32)
        all_ref[...] = scratch[...].astype(BF16)
        ids_copy.wait()
        blocks_copy.wait()
        for r in range(cands):
            live_ref[r : r + 1, :] = jnp.full((1, HD), BLOCK * blocks_ref[r])
        id_rows = [jnp.full((1, HD), ids_ref[r].astype(F32)) for r in range(cands)]
        id_rows = id_rows + [jnp.zeros((8 - cands, HD), F32)]
        for j in range(SLAB):
            first = (mine ^ j) * hq
            pieces = []
            for k in range(kvq):
                for r in range(cands):
                    at = pl.multiple_of(r * heads + first + k * group, 8)
                    pieces.append(scratch[pl.ds(at, group), :])
            part = jnp.concatenate(pieces + id_rows, axis=0).astype(BF16)
            if j < 2:
                (own_ref, near_ref)[j][...] = part
            else:
                far_ref[(j - 2) * part_rows : (j - 1) * part_rows, :] = part
        for copy in copies:
            copy.wait()

    hbm = pl.BlockSpec(memory_space=pl.ANY)
    out = pl.pallas_call(
        kernel,
        out_shape=[pltpu.VMEM((cands * heads, HD), BF16), pltpu.VMEM((8, HD), jnp.int32)]
        + [pltpu.VMEM((rows, HD), BF16) for rows in (part_rows, part_rows, 2 * part_rows)]
        + [pltpu.VMEM((2, prompts, span, kvw), BF16)] * 2,
        in_specs=[hbm] * 4,
        out_specs=[vmem_spec()] * 7,
        scratch_shapes=[
            pltpu.VMEM((cands, width), BF16),
            pltpu.SMEM((cands,), jnp.int32),
            pltpu.SMEM((cands,), jnp.int32),
            pltpu.VMEM((cands * heads, HD), F32),
            pltpu.SemaphoreType.DMA((3,)),
            pltpu.SemaphoreType.DMA((2, 2)),
        ],
        name="prepare",
    )(queries, prompt_of, blocks, prompt_cache)
    return out[0], out[1], out[2:5], out[5:]


def pack(own, near_part, far, passed):
    rows = own.shape[0]
    half = rows - 8

    def kernel(own_ref, near_ref, far_ref, passed_ref, out_ref):
        segment = lax.broadcasted_iota(jnp.int32, (8, HD), 1) // (HD // SLAB)
        ids = jnp.zeros((8, HD), F32)
        for j, (ref, at) in enumerate(((own_ref, 0), (near_ref, 0), (far_ref, 0), (passed_ref, rows))):
            out_ref[j * half : (j + 1) * half, :] = ref[at : at + half, :]
            ids = jnp.where(segment == j, ref[at + half : at + rows, :].astype(F32), ids)
        out_ref[SLAB * half :, :] = ids.astype(BF16)

    return pl.pallas_call(
        kernel,
        out_shape=pltpu.VMEM((SLAB * half + 8, HD), BF16),
        in_specs=[vmem_spec()] * 4,
        out_specs=vmem_spec(),
        name="pack",
    )(*near([own, near_part, far, passed]))


def suffix_attend(first, count, live, rows_q, suffix_cache, kv_heads, prompt_cache=None):
    cands, length, kv_width2 = suffix_cache.shape
    kv_width = kv_width2 // 2
    heads = rows_q.shape[0] // cands
    group = heads // kv_heads

    keeps = prompt_cache is not None
    if keeps:
        prompts, span, prompt_width2 = prompt_cache.shape
        prompt_width = prompt_width2 // 2
        kvw = prompt_width // SLAB

    def kernel(live_ref, q_ref, cache_ref, *rest):
        if keeps:
            prompt_ref, max_ref, sum_ref, mix_ref, *kv_refs, keys, values, sem, own_sem = rest
        else:
            max_ref, sum_ref, mix_ref, keys, values, sem = rest
        fetches = []
        for c in range(count):
            for side, target in enumerate((keys, values)):
                fetch = pltpu.make_async_copy(
                    cache_ref.at[first + c, :, side * kv_width : (side + 1) * kv_width],
                    target.at[c],
                    sem.at[c, side],
                )
                fetch.start()
                fetches.append(fetch)
        owns = []
        if keeps:
            mine = lax.axis_index("seq") % SLAB
            for j, ref in enumerate(kv_refs):
                for side in range(2):
                    column = pl.multiple_of(side * prompt_width + (mine ^ j) * kvw, kvw)
                    own = pltpu.make_async_copy(
                        prompt_ref.at[:, :, pl.ds(column, kvw)], ref.at[side], own_sem.at[j, side]
                    )
                    own.start()
                    owns.append(own)
        diagonal = (
            lax.broadcasted_iota(jnp.int32, (heads, kv_width), 0) // group
            == lax.broadcasted_iota(jnp.int32, (heads, kv_width), 1) // HD
        )
        position = lax.broadcasted_iota(jnp.int32, (heads, length), 1)
        for c in range(count):
            rows = slice(c * heads, (c + 1) * heads)
            held = first * heads
            wide = jnp.concatenate(
                [q_ref[held + c * heads : held + (c + 1) * heads, :]] * kv_heads, axis=1
            )
            wide = jnp.where(diagonal, wide, jnp.zeros_like(wide))
            fetches[2 * c].wait()
            logits = lax.dot_general(
                wide, keys[c], (((1,), (1,)), ((), ())), preferred_element_type=F32
            ) * HD ** (-0.5)
            live_row = jnp.concatenate([live_ref[first + c : first + c + 1, :]] * (length // HD), axis=1)
            live = position < live_row
            logits = jnp.where(live, logits, floor_logit)
            maxima = jnp.max(logits, axis=1, keepdims=True)
            exponent = jnp.where(live, jnp.exp(logits - maxima), 0.0)
            totals = jnp.sum(exponent, axis=1, keepdims=True)
            fetches[2 * c + 1].wait()
            mixed = jnp.dot(exponent.astype(BF16), values[c], preferred_element_type=F32)
            max_ref[rows, :] = jnp.broadcast_to(maxima, (heads, HD))
            sum_ref[rows, :] = jnp.broadcast_to(totals, (heads, HD))
            for k in range(kv_heads):
                at = c * heads + k * group
                mix_ref[at : at + group, :] = mixed[
                    k * group : (k + 1) * group, k * HD : (k + 1) * HD
                ]
        for own in owns:
            own.wait()

    hbm = pl.BlockSpec(memory_space=pl.ANY)
    extra = [pltpu.VMEM((2, prompts, span, kvw), BF16)] * 2 if keeps else []
    return pl.pallas_call(
        kernel,
        out_shape=[pltpu.VMEM((count * heads, HD), F32)] * 3 + extra,
        in_specs=[vmem_spec(), vmem_spec(), hbm] + [hbm] * keeps,
        out_specs=[vmem_spec()] * (3 + len(extra)),
        scratch_shapes=[
            pltpu.VMEM((count, length, kv_width), BF16),
            pltpu.VMEM((count, length, kv_width), BF16),
            pltpu.SemaphoreType.DMA((count, 2)),
        ]
        + [pltpu.SemaphoreType.DMA((2, 2))] * keeps,
        cost_estimate=pl.CostEstimate(
            flops=4 * count * heads * length * kv_width,
            transcendentals=count * heads * length,
            bytes_accessed=2 * suffix_cache.size * count // cands,
        ),
        name="suffix",
    )(*near([live, rows_q]), suffix_cache, *([prompt_cache] if keeps else []))


def prompt_attend(query_blocks, caches, cands, kvq, group):
    stacked = not isinstance(query_blocks, list)
    outer = query_blocks.shape[0] if stacked else len(query_blocks)
    chunk = math.gcd(outer, 4)
    part = cands * group
    part_rows = kvq * part
    block_rows = SLAB * part
    out_rows = kvq * block_rows + stat_rows(kvq)
    prompts, _ = caches[0].shape[1:3]

    def kernel(*refs):
        if stacked:
            q_refs = [refs[0].at[i] for i in range(chunk)]
            cache_refs = refs[1 : 1 + SLAB]
            out_refs = [refs[1 + SLAB].at[i] for i in range(chunk)]
        else:
            q_refs = refs[:chunk]
            cache_refs = refs[chunk : chunk + SLAB]
            out_refs = refs[chunk + SLAB :]
        rows = [q_ref[...].astype(F32) for q_ref in q_refs]
        ids = []
        segment = lax.broadcasted_iota(jnp.int32, (8, HD), 1) // (HD // SLAB)
        for i in range(chunk):
            for j in range(SLAB):
                mine = jnp.where(segment == j, rows[i][SLAB * part_rows :], 0.0)
                mine = jnp.max(mine, axis=1, keepdims=True)
                for r in range(cands):
                    ids.append(jnp.broadcast_to(mine[r : r + 1], (group, HD)))
        ids = jnp.concatenate(ids, axis=0)
        picked = [ids == float(p) for p in range(prompts)]
        stats = [[] for _ in range(chunk)]
        for k in range(kvq):
            q = jnp.concatenate(
                [
                    rows[i][j * part_rows + k * part : j * part_rows + (k + 1) * part]
                    for i in range(chunk)
                    for j in range(SLAB)
                ],
                axis=0,
            )
            q = jnp.concatenate([jnp.where(one, q, 0.0) for one in picked], axis=1).astype(BF16)

            def both(side):
                return jnp.concatenate(
                    [
                        jnp.concatenate(
                            [ref[side, p, :, k * HD : (k + 1) * HD] for p in range(prompts)], axis=1
                        )
                        for ref in cache_refs
                    ],
                    axis=0,
                )

            logits = lax.dot_general(
                q, both(0), (((1,), (1,)), ((), ())), preferred_element_type=F32
            ) * HD ** (-0.5)
            maxima = jnp.max(logits, axis=1, keepdims=True).astype(BF16).astype(F32)
            exponent = jnp.exp(logits - maxima)
            totals = jnp.sum(exponent, axis=1, keepdims=True)
            wide = jnp.dot(exponent.astype(BF16), both(1), preferred_element_type=F32)
            mixed = wide[:, :HD]
            for p in range(1, prompts):
                mixed = jnp.where(picked[p], wide[:, p * HD : (p + 1) * HD], mixed)
            for i in range(chunk):
                cut = slice(i * block_rows, (i + 1) * block_rows)
                out_refs[i][k * block_rows : (k + 1) * block_rows, :] = mixed[cut].astype(BF16)
                stats[i].append((to_lanes(maxima[cut]), to_lanes(totals[cut])))
        for i in range(chunk):
            out_refs[i][kvq * block_rows :, :] = pack_stats(stats[i]).astype(BF16)

    if stacked:
        whole = [
            pl.BlockSpec(c.shape, lambda s: (0, 0, 0, 0)) for c in caches
        ]
        return pl.pallas_call(
            kernel,
            out_shape=jax.ShapeDtypeStruct((outer, out_rows, HD), BF16),
            grid=(outer // chunk,),
            in_specs=[pl.BlockSpec((chunk, SLAB * part_rows + 8, HD), lambda s: (s, 0, 0))] + whole,
            out_specs=pl.BlockSpec((chunk, out_rows, HD), lambda s: (s, 0, 0)),
            name="prompt",
        )(query_blocks, *caches)
    return pl.pallas_call(
        kernel,
        out_shape=[pltpu.VMEM((out_rows, HD), BF16)] * outer,
        in_specs=[vmem_spec()] * (outer + SLAB),
        out_specs=[vmem_spec()] * outer,
        name="prompt",
    )(*near(query_blocks), *near(caches))


def merge(blocks, cands, kvq, group):
    stacked = not isinstance(blocks, list)
    outer = blocks.shape[0] if stacked else len(blocks)
    part = cands * group
    block_rows = SLAB * part
    out_rows = kvq * part + stat_rows(kvq)

    def kernel(*refs):
        if stacked:
            in_refs = [refs[0].at[i] for i in range(outer)]
            out_refs = refs[1:]
        else:
            in_refs = refs[:outer]
            out_refs = refs[outer:]
        stats = [ref[kvq * block_rows :, :].astype(F32) for ref in in_refs]
        merged = []
        for k in range(kvq):
            pairs = [unpack_stats(one, k) for one in stats]
            joined = pairs[0][0]
            for maximum, total in pairs[1:]:
                joined = jnp.maximum(joined, maximum)
            total_all = jnp.zeros((1, HD), F32)
            mixed = jnp.zeros((block_rows, HD), F32)
            for (maximum, total), ref in zip(pairs, in_refs):
                factor = jnp.exp(maximum - joined)
                total_all = total_all + factor * total
                mixed = mixed + to_rows(factor, block_rows, 0) * ref[
                    k * block_rows : (k + 1) * block_rows, :
                ].astype(F32)
            merged.append((joined, total_all))
            for j in range(SLAB):
                out_refs[j][k * part : (k + 1) * part, :] = mixed[
                    j * part : (j + 1) * part
                ].astype(BF16)
        packed = pack_stats(merged).astype(BF16)
        for j in range(SLAB):
            out_refs[j][kvq * part :, :] = packed

    args = [blocks] if stacked else blocks
    return pl.pallas_call(
        kernel,
        out_shape=[pltpu.VMEM((out_rows, HD), BF16)] * SLAB,
        in_specs=[vmem_spec()] * len(args),
        out_specs=[vmem_spec()] * SLAB,
        name="merge",
    )(*near(args))


def finish(pieces, suffix_state, reward, cands, kvq, group):
    part = cands * group
    hq = kvq * group
    heads = SLAB * hq

    def kernel(*refs):
        piece_refs = refs[:SLAB]
        state_refs = refs[SLAB : SLAB + len(suffix_state)]
        reward_ref, out_ref, score_ref, scratch = refs[SLAB + len(suffix_state) :]
        split = suffix_state[0].shape[0] // heads
        mine = lax.axis_index("seq") % SLAB
        scores = [jnp.zeros((group, HD), F32) for _ in range(cands)]
        for j in range(SLAB):
            first = (mine ^ j) * hq
            piece = piece_refs[j][...].astype(F32)
            mix, stats = piece[: kvq * part], piece[kvq * part :]
            for k in range(kvq):
                maximum, total = unpack_stats(stats, k)
                maximum = to_rows(maximum, part, j * part)
                total = to_rows(total, part, j * part)
                weight = reward_ref[pl.ds(pl.multiple_of(first + k * group, 8), group), :]
                for r in range(cands):
                    base = r * heads if r < split else (r - split) * heads
                    max_ref, sum_ref, mix_ref = state_refs[:3] if r < split else state_refs[3:]
                    row = pl.ds(pl.multiple_of(r * heads + first + k * group, 8), group)
                    at = pl.ds(pl.multiple_of(base + first + k * group, 8), group)
                    cut = slice(r * group, (r + 1) * group)
                    home_max = max_ref[at, :]
                    here_max = jnp.broadcast_to(maximum[cut], (group, HD))
                    joined = jnp.maximum(home_max, here_max)
                    home = jnp.exp(home_max - joined)
                    here = jnp.exp(here_max - joined)
                    total_all = home * sum_ref[at, :] + here * total[cut]
                    mixed = home * mix_ref[at, :] + here * mix[k * part :][cut]
                    attended = (mixed / total_all).astype(BF16).astype(F32)
                    scratch[row, :] = attended
                    scores[r] = scores[r] + attended * weight
        for h in range(heads):
            out_ref[:, h * HD : (h + 1) * HD] = scratch[pl.ds(h, cands, stride=heads), :].astype(
                BF16
            )
        for r in range(cands):
            score_ref[r] = jnp.sum(scores[r])

    smem = pl.BlockSpec(memory_space=pltpu.SMEM)
    return pl.pallas_call(
        kernel,
        out_shape=[
            jax.ShapeDtypeStruct((cands, heads * HD), BF16),
            jax.ShapeDtypeStruct((cands,), F32),
        ],
        in_specs=[vmem_spec()] * (SLAB + len(suffix_state) + 1),
        out_specs=[vmem_spec(), smem],
        scratch_shapes=[pltpu.VMEM((cands * heads, HD), F32)],
        name="finish",
    )(*near(pieces), *near(suffix_state), *near([reward]))


def attend(queries, prompt_of, suffix_cache, suffix_blocks, prompt_cache, reward_weight):
    cands = queries.shape[0]
    heads = queries.shape[1] // HD
    kv_heads = prompt_cache.shape[2] // (2 * HD)
    group = heads // kv_heads
    kvq = kv_heads // SLAB
    devices = lax.axis_size("seq")
    outer = devices // SLAB

    def hop(x, step):
        return lax.ppermute(x, "seq", [(i, i ^ step) for i in range(devices)])

    def spread(arrays, step):
        return [arrays[0]] + [hop(arrays[i], step * i) for i in range(1, len(arrays))]

    def relay(own, near_part, far_part):
        far = hop(far_part, 2)
        return [own, hop(near_part, 1), far, hop(far, 1)]

    direct = is_direct(devices)
    columns = [[SLAB * z + i for z in range(outer)] for i in range(SLAB)]

    rows_q, live, q_parts, kv_parts = prepare(
        queries, prompt_of[:, 0], suffix_blocks, prompt_cache, kvq, group
    )
    far_kv = [hop(kv_parts[j], 2 + j) for j in range(2)]
    own, near_q, far_q, passed_q = relay(*q_parts)
    q_slab = pack(own, near_q, far_q, passed_q)
    early = (cands + 2) // 3
    *state, own_kv, near_kv = suffix_attend(
        0, early, live, rows_q, suffix_cache, kv_heads, prompt_cache
    )
    state += suffix_attend(early, cands - early, live, rows_q, suffix_cache, kv_heads)
    kv_parts = [own_kv, hop(near_kv, 1)] + far_kv
    if direct:
        q_all = spread([q_slab] * outer, SLAB)
    else:
        q_all = lax.all_gather(q_slab, "seq", axis_index_groups=columns)
    partial = prompt_attend(q_all, kv_parts, cands, kvq, group)
    if direct:
        partial = spread(partial, SLAB)
    else:
        partial = lax.all_to_all(
            partial, "seq", split_axis=0, concat_axis=0, axis_index_groups=columns, tiled=True
        )
    pieces = spread(merge(partial, cands, kvq, group), 1)
    reward = reward_weight.reshape(heads, HD)
    return tuple(finish(pieces, state, reward, cands, kvq, group))


def is_direct(devices):
    outer = devices // SLAB
    return outer == 4


def solution(mesh):
    placed = (
        P(("groups", "seq"), None),
        P(("groups", "seq"), None),
        P(("groups", "seq"), None, None),
        P(("groups", "seq")),
        P("groups", "seq", None),
        P(),
    )
    return jax.shard_map(
        attend,
        mesh=mesh,
        in_specs=placed,
        out_specs=(P(("groups", "seq"), None), P(("groups", "seq"))),
        check_vma=False,
    )
```
